32 devices in a mesh: clip: 2 (over y), tm: 4 (over z), band: 2 (over x), head: 2 (over core).
Axes of the slice: x: 2, y: 2, z: 4, core: 2. Of those that a mesh axis runs over, the one named last changes fastest.
Arguments:
- queries: bfloat16 [8, 2, 256, 1536], P(('clip', 'tm'), 'band', None, 'head'), parts along dimension 0, may hold values from -6 to 6
- keys: bfloat16 [8, 2, 256, 1536], P(('clip', 'tm'), 'band', None, 'head'), parts along dimension 0, may hold values from -6 to 6
- values: bfloat16 [8, 2, 256, 1536], P(('clip', 'tm'), 'band', None, 'head'), parts along dimension 0, may hold values from -6 to 6
- adj_mask: int32 [8, 2, 2, 2], P(('clip', 'tm'), 'band'), parts along dimension 0, may hold values from 0 to 1, as said below
- border_blocks: int32 [8, 2, 2, 1], P(('clip', 'tm'), 'band'), parts along dimension 0, may hold values from 0 to 1
Outputs:
- attended: bfloat16 [8, 2, 256, 1536], P(('clip', 'tm'), 'band', None, 'head'), parts along dimension 0
The draws below stay inside these ranges and needn't reach their ends.
There are 2 independent parts, one for each index of `clip`. The reference program is written for one: setup_inputs(seed, part) draws one part's arguments, and reference() takes and returns one part's arrays. A program takes and returns all parts, laid end to end along the dimension named above; each array names one. Nothing has to cross between parts.
Inputs may be any that keep to these rules, and one draw needn't show every extreme that they name: `adj_mask`: for each slab, band and direction exactly 1 of the 2 entries are 1.
All inputs are finite; a program needn't handle non-finite values.
Results may differ from the reference program's by a relative error of at most 0.0043.
Values may be sent and summed in bfloat16 or wider, within the bound.
A program may use at most 64 MiB of HBM per device.

```python
import math
import jax
import jax.numpy as jnp
from jax import lax

SLABS = 4
BANDS = 2
ROWS = 256
BLK = 128
KB = 2
BSEL = 1
HEADS = 12
HD = 128


def draw_pair(key):
    array_shape = (SLABS, BANDS, ROWS, HEADS * HD)
    first_key, second_key = jax.random.split(key, 2)
    query_field = jnp.clip(jax.random.normal(first_key, array_shape, jnp.float32), -6.0, 6.0)
    key_field = jnp.clip(jax.random.normal(second_key, array_shape, jnp.float32), -6.0, 6.0)
    return (query_field, key_field)


def draw_queries(key, part):
    return draw_pair(jax.random.fold_in(key, 11))[0].astype(jnp.bfloat16)


def draw_keys(key, part):
    return draw_pair(jax.random.fold_in(key, 11))[1].astype(jnp.bfloat16)


def block_orders(key):
    streams = jax.random.split(key, SLABS * BANDS * 2)
    return jax.vmap(lambda stream: jax.random.permutation(stream, KB))(streams)


def draw_adj_mask(key, part):
    orders = block_orders(jax.random.fold_in(key, 23))
    return (orders < KB // 2).astype(jnp.int32).reshape(SLABS, BANDS, 2, KB)


def draw_border_blocks(key, part):
    orders = block_orders(jax.random.fold_in(key, 37))
    return orders[:, :BSEL].astype(jnp.int32).reshape(SLABS, BANDS, 2, BSEL)


def levels(key, extent, cuts, low, high):
    level, own = 1.0, jax.random.fold_in(key, 6)
    for dim, shards_of in cuts:
        heights = jnp.exp(jax.random.uniform(jax.random.fold_in(own, dim), (shards_of,), jnp.float32, low / len(cuts), high / len(cuts)))
        level = level * jnp.repeat(heights, extent[dim] // shards_of).reshape([-1 if axis == dim else 1 for axis in range(len(extent))])
    return level


def normal_values(rng, dims, deviation, most, cuts=(), kind=jnp.bfloat16):
    values = deviation * jax.random.normal(rng, dims, jnp.float32)
    if cuts:
        values = values * levels(rng, dims, cuts, -0.22, 0.18)
    return jnp.clip(values, -most, most).astype(kind)


def setup_inputs(seed: int = 0, part: int = 0) -> dict:
    seeds = jax.random.split(jax.random.key(seed), 6)
    part_keys = jax.random.split(jax.random.fold_in(seeds[5], part), 6)
    queries = draw_queries(jax.random.fold_in(jax.random.fold_in(seeds[5], part), 71), part)
    keys = draw_keys(jax.random.fold_in(jax.random.fold_in(seeds[5], part), 71), part)
    values = normal_values(part_keys[2], (SLABS, BANDS, ROWS, HEADS * HD), 1.0, 6.0, ((0, 4), (1, 2), (3, 2)))
    adj_mask = draw_adj_mask(jax.random.fold_in(jax.random.fold_in(seeds[5], part), 71), part)
    border_blocks = draw_border_blocks(jax.random.fold_in(jax.random.fold_in(seeds[5], part), 71), part)
    return dict(queries=queries, keys=keys, values=values, adj_mask=adj_mask, border_blocks=border_blocks)


masked_score = -1e+30

def attend(query_rows, key_rows, value_rows, bias):
    query_heads = query_rows.reshape(query_rows.shape[0], HEADS, HD).astype(jnp.float32)
    key_heads = key_rows.reshape(key_rows.shape[0], HEADS, HD).astype(jnp.float32)
    value_heads = value_rows.reshape(value_rows.shape[0], HEADS, HD).astype(jnp.float32)
    scores = jnp.einsum('qhd,khd->hqk', query_heads, key_heads) * (1.0 / math.sqrt(HD)) + bias
    maxima = lax.optimization_barrier(jnp.max(scores, axis=2))
    weights = jnp.exp(scores - maxima[:, :, None])
    totals = lax.optimization_barrier(jnp.sum(weights, axis=2))
    rounded = lax.optimization_barrier(weights.astype(jnp.bfloat16)).astype(jnp.float32)
    output = jnp.einsum('hqk,khd->qhd', rounded, value_heads)
    return (maxima, totals, output)

def combine_sources(pieces):
    maxima = jnp.stack([piece[0] for piece in pieces])
    largest = lax.optimization_barrier(jnp.max(maxima, axis=0))
    factors = jnp.exp(maxima - largest)
    numerator = factors[0].T[:, :, None] * pieces[0][2]
    for number in range(1, len(pieces)):
        numerator = numerator + factors[number].T[:, :, None] * pieces[number][2]
    denominator = lax.optimization_barrier(jnp.sum(factors * jnp.stack([piece[1] for piece in pieces]), axis=0))
    return numerator / denominator.T[:, :, None]

def reference(queries, keys, values, adj_mask, border_blocks):

    def one_device(device_index):
        slab_index = device_index // BANDS
        band_index = device_index % BANDS
        prev_slab = jnp.maximum(slab_index - 1, 0)
        next_slab = jnp.minimum(slab_index + 1, SLABS - 1)
        lower_band = jnp.maximum(band_index - 1, 0)
        upper_band = jnp.minimum(band_index + 1, BANDS - 1)
        query_rows = queries[slab_index, band_index]
        own_piece = attend(query_rows, keys[slab_index, band_index], values[slab_index, band_index], jnp.zeros((ROWS,), jnp.float32))
        prev_bias = jnp.where(jnp.repeat(adj_mask[prev_slab, band_index, 0] == 1, BLK) & (slab_index > 0), 0.0, masked_score).astype(jnp.float32)
        prev_piece = attend(query_rows, keys[prev_slab, band_index], values[prev_slab, band_index], prev_bias)
        next_bias = jnp.where(jnp.repeat(adj_mask[next_slab, band_index, 1] == 1, BLK) & (slab_index < SLABS - 1), 0.0, masked_score).astype(jnp.float32)
        next_piece = attend(query_rows, keys[next_slab, band_index], values[next_slab, band_index], next_bias)

        def picked_rows(source, band_from, direction):
            chosen = border_blocks[slab_index, band_from, direction]
            return source[slab_index, band_from].reshape(KB, BLK, HEADS * HD)[chosen].reshape(BSEL * BLK, HEADS * HD)
        rim_rows = BSEL * BLK
        lower_bias = jnp.where(band_index > 0, jnp.zeros((rim_rows,), jnp.float32), jnp.full((rim_rows,), masked_score, jnp.float32))
        upper_bias = jnp.where(band_index < BANDS - 1, jnp.zeros((rim_rows,), jnp.float32), jnp.full((rim_rows,), masked_score, jnp.float32))
        lower_piece = attend(query_rows, picked_rows(keys, lower_band, 1), picked_rows(values, lower_band, 1), lower_bias)
        upper_piece = attend(query_rows, picked_rows(keys, upper_band, 0), picked_rows(values, upper_band, 0), upper_bias)
        merged = combine_sources([own_piece, prev_piece, next_piece, lower_piece, upper_piece])
        return merged.reshape(ROWS, HEADS * HD).astype(jnp.bfloat16)
    results = lax.map(one_device, jnp.arange(SLABS * BANDS, dtype=jnp.int32))
    return results.reshape(SLABS, BANDS, ROWS, HEADS * HD)
```

```python
import functools
import math

import jax
import jax.numpy as jnp
from jax import lax
from jax.experimental import pallas as pl
from jax.experimental.pallas import tpu as pltpu
from jax.sharding import PartitionSpec as P

BLK = 128
HD = 128

masked_score = -1e30
SCALE2 = math.log2(math.e) / math.sqrt(HD)
MESH = pl.DeviceIdType.MESH


def routes(slab_count, band_count):
    slab, band = lax.axis_index("tm"), lax.axis_index("band")
    found = []
    if slab_count > 1:
        found.append(({"tm": slab + 1}, slab < slab_count - 1, None, slab > 0, ("adj", 0)))
        found.append(({"tm": slab - 1}, None, slab > 0, slab < slab_count - 1, ("adj", 1)))
    if band_count == 2:
        found.append(({"band": 1 - band}, band == 0, band == 1, None, ("border", 1 - band)))
    elif band_count > 2:
        found.append(({"band": band + 1}, band < band_count - 1, None, band > 0, ("border", 1)))
        found.append(({"band": band - 1}, None, band > 0, band < band_count - 1, ("border", 0)))
    return found


def when(condition):
    return (lambda body: body()) if condition is None else pl.when(condition)


def chunks_of(heads):
    return (
        [(0, heads)],
        [(0, heads - 1), (heads - 1, 1)],
    )


def weigh(query, key):
    scores = lax.dot_general(
        query, key, (((1,), (1,)), ((), ())), preferred_element_type=jnp.float32
    )
    return scores * SCALE2


def kernel(
    slab_count, band_count, q_hbm, k_hbm, v_hbm, adj_hbm, border_hbm, out_ref,
    q_ref, k_ref, v_ref, adj_ref, border_ref, send_ref, recv_ref, acc_ref, weights_ref,
    gain_ref, load_sem, here_sem, send_sem, recv_sem,
):
    plan = routes(slab_count, band_count)
    rows, width = q_ref.shape
    heads = width // HD

    neighbours = []
    for axis, count in (("tm", slab_count), ("band", band_count)):
        if count > 1:
            index = lax.axis_index(axis)
            neighbours.append((axis, index, index > 0, index < count - 1))

    barrier = pltpu.get_barrier_semaphore()
    for axis, index, _, has_upper in neighbours:
        @pl.when(has_upper)
        def _():
            pl.semaphore_signal(barrier, inc=1, device_id={axis: index + 1}, device_id_type=MESH)

    picks = []
    for number, (source, target) in enumerate(((adj_hbm, adj_ref), (border_hbm, border_ref))):
        picks.append(pltpu.make_async_copy(source, target, load_sem.at[number]))
    for pick in picks:
        pick.start()
    loads = [
        pltpu.make_async_copy(source, target, load_sem.at[2 + number])
        for number, (source, target) in enumerate(((k_hbm, k_ref), (v_hbm, v_ref), (q_hbm, q_ref)))
    ]
    for load in loads:
        load.start()

    chunks = chunks_of(heads)

    def transfer(slot, part, group):
        at = (slot, part, pl.ds(*chunks[part][group]))
        return pltpu.make_async_remote_copy(
            src_ref=send_ref.at[at],
            dst_ref=recv_ref.at[at],
            send_sem=send_sem.at[slot, part, group],
            recv_sem=recv_sem.at[slot, part, group],
            device_id=plan[slot][0],
            device_id_type=MESH,
        )

    def send(part, downward):
        for group in range(len(chunks[part])):
            for slot, (_, up, down, _, _) in enumerate(plan):
                sends = down if downward else up
                if sends is not None:
                    @pl.when(sends)
                    def _():
                        transfer(slot, part, group).start()

    arrivals = sum(lower.astype(jnp.int32) for _, _, lower, _ in neighbours)

    @pl.when(arrivals > 0)
    def _():
        pl.semaphore_wait(barrier, arrivals)

    for number, (axis, index, has_lower, _) in enumerate(neighbours):
        @pl.when(has_lower)
        def _():
            pl.semaphore_signal(
                here_sem.at[number], inc=1, device_id={axis: index - 1}, device_id_type=MESH
            )

    for pick in picks:
        pick.wait()
    blocks = [
        adj_ref[row, 1] if kind == "adj" else border_ref[0, row] for _, _, _, _, (kind, row) in plan
    ]
    late = lax.axis_index("head") > 0
    for part, whole in enumerate((k_ref, v_ref)):
        loads[part].wait()
        for slot in range(len(plan)):
            for head in range(heads):
                send_ref[slot, part, head] = whole[blocks[slot], :, head * HD : (head + 1) * HD]
        if part == 0:
            send(0, True)
            for number, (_, _, _, has_upper) in enumerate(neighbours):
                @pl.when(has_upper)
                def _():
                    pl.semaphore_wait(here_sem.at[number], 1)
            send(0, False)
    @pl.when(jnp.logical_not(late))
    def _():
        send(1, True)
        send(1, False)

    for slot, (_, _, _, comes, _) in enumerate(plan):
        if comes is not None:
            @pl.when(jnp.logical_not(comes))
            def _():
                recv_ref[slot] = jnp.zeros(recv_ref.shape[1:], recv_ref.dtype)

    loads[2].wait()
    own = []
    for head in range(heads):
        columns = slice(head * HD, (head + 1) * HD)
        scores = weigh(q_ref[:, columns], k_ref[:, :, columns].reshape(rows, HD))
        most = jnp.max(scores, axis=1, keepdims=True)
        weights = jnp.exp2(scores - most)
        total = jnp.sum(weights, axis=1, keepdims=True)
        acc_ref[head] = jnp.dot(
            weights.astype(jnp.bfloat16), v_ref[:, :, columns].reshape(rows, HD), preferred_element_type=jnp.float32
        )
        own.append((most, total))

    for group, (start, size) in enumerate(chunks[0]):
        for slot, (_, _, _, comes, _) in enumerate(plan):
            @when(comes)
            def _():
                transfer(slot, 0, group).wait_recv()
        @pl.when(late)
        def _():
            send(1, True)
            send(1, False)

        for head in range(start, start + size):
            columns = slice(head * HD, (head + 1) * HD)
            pieces = [own[head]]
            for slot, (_, _, _, comes, _) in enumerate(plan):
                scores = weigh(q_ref[:, columns], recv_ref[slot, 0, head])
                if comes is not None:
                    scores = scores + jnp.where(comes, 0.0, masked_score).astype(jnp.float32)
                most = jnp.max(scores, axis=1, keepdims=True)
                weights = jnp.exp2(scores - most)
                total = jnp.sum(weights, axis=1, keepdims=True)
                weights_ref[head, slot] = weights.astype(jnp.bfloat16)
                pieces.append((most, total))
            largest = functools.reduce(jnp.maximum, [most for most, _ in pieces])
            factors = [jnp.exp2(most - largest) for most, _ in pieces]
            denominator = sum(factor * total for factor, (_, total) in zip(factors, pieces))
            acc_ref[head] = acc_ref[head] * (factors[0] / denominator)
            for slot in range(len(plan)):
                gain_ref[head, slot] = jnp.broadcast_to(
                    factors[slot + 1] / denominator, (rows, HD)
                )

    for group, (start, size) in enumerate(chunks[1]):
        for slot, (_, _, _, comes, _) in enumerate(plan):
            @when(comes)
            def _():
                transfer(slot, 1, group).wait_recv()
        for head in range(start, start + size):
            result = acc_ref[head]
            for slot in range(len(plan)):
                result = result + gain_ref[head, slot] * jnp.dot(
                    weights_ref[head, slot], recv_ref[slot, 1, head], preferred_element_type=jnp.float32
                )
            out_ref[:, head * HD : (head + 1) * HD] = result.astype(out_ref.dtype)

    for part in range(2):
        for group in range(len(chunks[part])):
            for slot, (_, up, down, _, _) in enumerate(plan):
                sends = down if up is None else up if down is None else None

                @when(sends)
                def _():
                    transfer(slot, part, group).wait_send()


def per_device(queries, keys, values, adj_mask, border_blocks):
    rows, width = queries.shape[2:]
    heads = width // HD
    slab_count, band_count = lax.axis_size("tm"), lax.axis_size("band")
    sources = (2 if slab_count > 1 else 0) + min(band_count - 1, 2)
    assert rows == 2 * BLK and adj_mask.shape[3] == 2 and border_blocks.shape[3] == 1
    block_sems = pltpu.SemaphoreType.DMA((sources, 2, max(map(len, chunks_of(heads)))))
    attended = pl.pallas_call(
        functools.partial(kernel, slab_count, band_count),
        out_shape=pltpu.VMEM((rows, width), jnp.bfloat16),
        in_specs=[pl.BlockSpec(memory_space=pl.ANY)] * 5,
        out_specs=pl.BlockSpec(memory_space=pltpu.VMEM),
        scratch_shapes=[
            pltpu.VMEM((rows, width), jnp.bfloat16),
            pltpu.VMEM((rows // BLK, BLK, width), jnp.bfloat16),
            pltpu.VMEM((rows // BLK, BLK, width), jnp.bfloat16),
            pltpu.SMEM(adj_mask.shape[2:], jnp.int32),
            pltpu.SMEM(border_blocks.shape[:1:-1], jnp.int32),
            pltpu.VMEM((sources, 2, heads, BLK, HD), jnp.bfloat16),
            pltpu.VMEM((sources, 2, heads, BLK, HD), jnp.bfloat16),
            pltpu.VMEM((heads, rows, HD), jnp.float32),
            pltpu.VMEM((heads, sources, rows, BLK), jnp.bfloat16),
            pltpu.VMEM((heads, sources, rows, HD), jnp.float32),
            pltpu.SemaphoreType.DMA((5,)),
            pltpu.SemaphoreType.REGULAR((max(1, (slab_count > 1) + (band_count > 1)),)),
            block_sems,
            block_sems,
        ],
        compiler_params=pltpu.CompilerParams(collective_id=0, has_side_effects=True),
        name="radial_attention",
    )(
        queries[0, 0],
        keys.reshape(rows // BLK, BLK, width),
        values.reshape(rows // BLK, BLK, width),
        adj_mask[0, 0], border_blocks[0, 0].T,
    )
    return attended[None, None]


def solution(mesh):
    placed = (
        P(("clip", "tm"), "band", None, "head"),
        P(("clip", "tm"), "band", None, "head"),
        P(("clip", "tm"), "band", None, "head"),
        P(("clip", "tm"), "band", None, None),
        P(("clip", "tm"), "band", None, None),
    )
    return jax.shard_map(
        per_device,
        mesh=mesh,
        in_specs=placed,
        out_specs=P(("clip", "tm"), "band", None, "head"),
        check_vma=False,
    )
```

```python
import functools
import math

import jax
import jax.numpy as jnp
from jax import lax
from jax.experimental import pallas as pl
from jax.experimental.pallas import tpu as pltpu
from jax.sharding import PartitionSpec as P

BLK = 128
HD = 128

masked_score = -1e30
SCALE2 = math.log2(math.e) / math.sqrt(HD)
MESH = pl.DeviceIdType.MESH


def routes(slab_count, band_count):
    slab, band = lax.axis_index("tm"), lax.axis_index("band")
    found = []
    if slab_count > 1:
        found.append(({"tm": slab - 1}, None, slab > 0, slab < slab_count - 1, ("adj", 1), slab < slab_count - 1))
    if band_count == 2:
        found.append(({"band": 1 - band}, band == 0, band == 1, None, ("border", 1 - band), band == 0))
    elif band_count > 2:
        found.append(({"band": band - 1}, None, band > 0, band < band_count - 1, ("border", 0), band < band_count - 1))
        found.append(({"band": band + 1}, band < band_count - 1, None, band > 0, ("border", 1), None))
    if slab_count > 1:
        found.append(({"tm": slab + 1}, slab < slab_count - 1, None, slab > 0, ("adj", 0), None))
    return found


def when(condition):
    return (lambda body: body()) if condition is None else pl.when(condition)


def value_chunks(heads):
    return [(0, (heads - 1) * BLK), ((heads - 1) * BLK, BLK)]


def ahead_parts(heads):
    return [(0, BLK)]


def weigh(query, key):
    scores = lax.dot_general(
        query, key, (((1,), (1,)), ((), ())), preferred_element_type=jnp.float32
    )
    return scores * SCALE2


def kernel(
    slab_count, band_count, q_hbm, k_hbm, v_hbm, adj_hbm, border_hbm, out_ref,
    q_ref, k_ref, v_ref, adj_ref, border_ref, send_ref, recv_ref, acc_ref, weights_ref,
    both_ref, peer_adj_ref, peer_border_ref,
    load_sem, here_sem, send_sem, recv_sem, ahead_send_sem, ahead_recv_sem,
):
    plan = routes(slab_count, band_count)
    slots = range(len(plan))
    rows, width = q_ref.shape
    heads = width // HD
    late = lax.axis_index("head") > 0
    early = jnp.logical_not(late)

    neighbours = []
    for axis, count in (("tm", slab_count), ("band", band_count)):
        if count > 1:
            index = lax.axis_index(axis)
            neighbours.append((axis, index, index > 0, index < count - 1))

    barrier = pltpu.get_barrier_semaphore()
    for axis, index, _, has_upper in neighbours:
        @pl.when(has_upper)
        def _():
            pl.semaphore_signal(barrier, inc=1, device_id={axis: index + 1}, device_id_type=MESH)

    loads = [
        pltpu.make_async_copy(source, target, load_sem.at[number])
        for number, (source, target) in enumerate(
            ((k_hbm, k_ref), (adj_hbm, adj_ref), (border_hbm, border_ref), (v_hbm, v_ref), (q_hbm, q_ref))
        )
    ]
    for load in loads[:3]:
        load.start()

    chunks = [[(0, heads * BLK)], value_chunks(heads)]
    pieces_ahead = ahead_parts(heads)
    skipped = sum(size for _, size in pieces_ahead)

    def transfer(slot, part, group, skip=0):
        start, size = chunks[part][group]
        at = (slot, part, pl.ds(start + skip, size - skip))
        return pltpu.make_async_remote_copy(
            src_ref=send_ref.at[at],
            dst_ref=recv_ref.at[at],
            send_sem=send_sem.at[slot, part, group],
            recv_sem=recv_sem.at[slot, part, group],
            device_id=plan[slot][0],
            device_id_type=MESH,
        )

    def ahead(slot):
        mask = (adj_hbm, peer_adj_ref) if plan[slot][4][0] == "adj" else (border_hbm, peer_border_ref)
        parts = [
            (k_hbm.at[:, pl.ds(0, size), pl.ds(head * HD, HD)], both_ref.at[slot, head, :, pl.ds(0, size)])
            for head, size in pieces_ahead
        ]
        return [
            pltpu.make_async_remote_copy(
                src_ref=source,
                dst_ref=target,
                send_sem=ahead_send_sem.at[slot, number],
                recv_sem=ahead_recv_sem.at[slot, number],
                device_id=plan[slot][0],
                device_id_type=MESH,
            )
            for number, (source, target) in enumerate(parts + [mask])
        ]

    def send(slot, part, downward):
        _, up, down, _, _, above = plan[slot]
        sends = down if downward else up
        if sends is None:
            return
        for group in range(len(chunks[part])):
            if downward and part == 0 and above is not None:
                @pl.when(sends & late)
                def _():
                    transfer(slot, part, group, skipped).start()

                @pl.when(sends & early)
                def _():
                    transfer(slot, part, group).start()
            else:
                @pl.when(sends)
                def _():
                    transfer(slot, part, group).start()

    arrivals = sum(lower.astype(jnp.int32) for _, _, lower, _ in neighbours)

    @pl.when(arrivals > 0)
    def _():
        pl.semaphore_wait(barrier, arrivals)

    for slot, (_, _, down, _, _, above) in enumerate(plan):
        if above is not None:
            @pl.when(down & late)
            def _():
                for copy in ahead(slot):
                    copy.start()

    for number, (axis, index, has_lower, _) in enumerate(neighbours):
        @pl.when(has_lower)
        def _():
            pl.semaphore_signal(
                here_sem.at[number], inc=1, device_id={axis: index - 1}, device_id_type=MESH
            )

    for load in loads[3:]:
        load.start()
    for load in loads[1:3]:
        load.wait()
    blocks = [
        adj_ref[row, 1] if kind == "adj" else border_ref[0, row] for _, _, _, _, (kind, row), _ in plan
    ]

    def pick(slot, part, whole):
        for head in range(heads):
            send_ref[slot, part, head * BLK : (head + 1) * BLK] = whole[
                blocks[slot], :, head * HD : (head + 1) * HD
            ]

    loads[0].wait()
    for slot in slots:
        pick(slot, 0, k_ref)
        send(slot, 0, True)
    for number, (_, _, _, has_upper) in enumerate(neighbours):
        @pl.when(has_upper)
        def _():
            pl.semaphore_wait(here_sem.at[number], 1)
    for slot in slots:
        send(slot, 0, False)

    loads[3].wait()
    for slot in slots:
        pick(slot, 1, v_ref)

    def send_values():
        for slot in slots:
            send(slot, 1, True)
            send(slot, 1, False)

    pl.when(early)(send_values)

    for slot, (_, _, _, comes, _, _) in enumerate(plan):
        if comes is not None:
            @pl.when(jnp.logical_not(comes))
            def _():
                recv_ref[slot] = jnp.zeros(recv_ref.shape[1:], recv_ref.dtype)

    loads[4].wait()
    own = []
    for head in range(heads):
        columns = slice(head * HD, (head + 1) * HD)
        scores = weigh(q_ref[:, columns], k_ref[:, :, columns].reshape(rows, HD))
        most = jnp.max(scores, axis=1, keepdims=True)
        weights = jnp.exp2(scores - most)
        total = jnp.sum(weights, axis=1, keepdims=True)
        acc_ref[head] = jnp.dot(
            weights.astype(jnp.bfloat16), v_ref[:, :, columns].reshape(rows, HD), preferred_element_type=jnp.float32
        )
        own.append((most, total))

    for slot, (*_, above) in enumerate(plan):
        if above is not None:
            @pl.when(above & late)
            def _():
                for copy in ahead(slot):
                    copy.wait_recv()

    for slot, (_, _, _, comes, (kind, _), above) in enumerate(plan):
        if above is None:
            @when(comes)
            def _():
                transfer(slot, 0, 0).wait_recv()
        else:
            @pl.when(above & late)
            def _():
                block = peer_adj_ref[1, 1] if kind == "adj" else peer_border_ref[0, 0]
                for head, size in pieces_ahead:
                    recv_ref[slot, 0, head * BLK : head * BLK + size] = both_ref[slot, head, block, :size]
                transfer(slot, 0, 0, skipped).wait_recv()

            whole = jnp.logical_not(above & late)

            @pl.when(whole if comes is None else whole & comes)
            def _():
                transfer(slot, 0, 0).wait_recv()

    pl.when(late)(send_values)

    def arrived(part, head):
        return jnp.concatenate(
            [recv_ref[slot, part, head * BLK : (head + 1) * BLK] for slot in slots], axis=0
        )

    hidden = [
        None if comes is None else jnp.where(comes, 0.0, masked_score).astype(jnp.float32)
        for _, _, _, comes, _, _ in plan
    ]
    for head in range(heads):
        columns = slice(head * HD, (head + 1) * HD)
        scores = weigh(q_ref[:, columns], arrived(0, head))
        scores = [
            scores[:, slot * BLK : (slot + 1) * BLK] + (0.0 if hidden[slot] is None else hidden[slot]) for slot in slots
        ]
        most, total = own[head]
        largest = jnp.maximum(
            most, jnp.max(functools.reduce(jnp.maximum, scores), axis=1, keepdims=True)
        )
        weights = [jnp.exp2(score - largest) for score in scores]
        factor = jnp.exp2(most - largest)
        share = 1.0 / (factor * total + jnp.sum(sum(weights), axis=1, keepdims=True))
        acc_ref[head] = acc_ref[head] * (factor * share)
        for slot in slots:
            weights_ref[head, :, slot * BLK : (slot + 1) * BLK] = (weights[slot] * share).astype(jnp.bfloat16)

    for group, (start, size) in enumerate(chunks[1]):
        for slot, (_, _, _, comes, _, _) in enumerate(plan):
            @when(comes)
            def _():
                transfer(slot, 1, group).wait_recv()
        for head in range(start // BLK, (start + size) // BLK):
            result = acc_ref[head] + jnp.dot(
                weights_ref[head], arrived(1, head), preferred_element_type=jnp.float32
            )
            out_ref[:, head * HD : (head + 1) * HD] = result.astype(out_ref.dtype)

    for slot, (_, up, down, _, _, above) in enumerate(plan):
        sends = down if up is None else up if down is None else None
        if above is None:
            @when(sends)
            def _():
                transfer(slot, 0, 0).wait_send()
        else:
            @pl.when(down & late)
            def _():
                for copy in ahead(slot):
                    copy.wait_send()
                transfer(slot, 0, 0, skipped).wait_send()

            whole = jnp.logical_not(down & late)

            @pl.when(whole if sends is None else whole & sends)
            def _():
                transfer(slot, 0, 0).wait_send()
        for group in range(len(chunks[1])):
            @when(sends)
            def _():
                transfer(slot, 1, group).wait_send()


def per_device(queries, keys, values, adj_mask, border_blocks):
    rows, width = queries.shape[2:]
    heads = width // HD
    slab_count, band_count = lax.axis_size("tm"), lax.axis_size("band")
    sources = (2 if slab_count > 1 else 0) + min(band_count - 1, 2)
    assert rows == 2 * BLK and adj_mask.shape[3] == 2 and border_blocks.shape[3] == 1
    pieces = len(ahead_parts(heads))
    block_sems = pltpu.SemaphoreType.DMA((sources, 2, len(value_chunks(heads))))
    ahead_sems = pltpu.SemaphoreType.DMA((sources, pieces + 1))
    attended = pl.pallas_call(
        functools.partial(kernel, slab_count, band_count),
        out_shape=pltpu.VMEM((rows, width), jnp.bfloat16),
        in_specs=[pl.BlockSpec(memory_space=pl.ANY)] * 5,
        out_specs=pl.BlockSpec(memory_space=pltpu.VMEM),
        scratch_shapes=[
            pltpu.VMEM((rows, width), jnp.bfloat16),
            pltpu.VMEM((rows // BLK, BLK, width), jnp.bfloat16),
            pltpu.VMEM((rows // BLK, BLK, width), jnp.bfloat16),
            pltpu.SMEM(adj_mask.shape[2:], jnp.int32),
            pltpu.SMEM(border_blocks.shape[:1:-1], jnp.int32),
            pltpu.VMEM((sources, 2, heads * BLK, HD), jnp.bfloat16),
            pltpu.VMEM((sources, 2, heads * BLK, HD), jnp.bfloat16),
            pltpu.VMEM((heads, rows, HD), jnp.float32),
            pltpu.VMEM((heads, rows, sources * BLK), jnp.bfloat16),
            pltpu.VMEM((sources, pieces, rows // BLK, BLK, HD), jnp.bfloat16),
            pltpu.SMEM(adj_mask.shape[2:], jnp.int32),
            pltpu.SMEM(border_blocks.shape[:1:-1], jnp.int32),
            pltpu.SemaphoreType.DMA((5,)),
            pltpu.SemaphoreType.REGULAR((max(1, (slab_count > 1) + (band_count > 1)),)),
            block_sems,
            block_sems,
            ahead_sems,
            ahead_sems,
        ],
        compiler_params=pltpu.CompilerParams(collective_id=0, has_side_effects=True),
        name="radial_attention",
    )(
        queries[0, 0],
        keys.reshape(rows // BLK, BLK, width),
        values.reshape(rows // BLK, BLK, width),
        adj_mask[0, 0], border_blocks[0, 0].T,
    )
    return attended[None, None]


def solution(mesh):
    placed = (
        P(("clip", "tm"), "band", None, "head"),
        P(("clip", "tm"), "band", None, "head"),
        P(("clip", "tm"), "band", None, "head"),
        P(("clip", "tm"), "band", None, None),
        P(("clip", "tm"), "band", None, None),
    )
    return jax.shard_map(
        per_device,
        mesh=mesh,
        in_specs=placed,
        out_specs=P(("clip", "tm"), "band", None, "head"),
        check_vma=False,
    )
```

```python
import functools
import math

import jax
import jax.numpy as jnp
from jax import lax
from jax.experimental import pallas as pl
from jax.experimental.pallas import tpu as pltpu
from jax.sharding import PartitionSpec as P

BLK = 128
HD = 128

masked_score = -1e30
SCALE2 = math.log2(math.e) / math.sqrt(HD)
MESH = pl.DeviceIdType.MESH

ROUTE_X = ((0, 0, 1), (1, 0, 1))
ROUTE_Z = ((0, 1, 0), (1, 1, 0))


def routes(slab_count, band_count):
    slab, band = lax.axis_index("tm"), lax.axis_index("band")
    found = []
    if slab_count > 1:
        found.append(({"tm": slab - 1}, None, slab > 0, slab < slab_count - 1, ("adj", 1), slab < slab_count - 1))
    if band_count == 2:
        found.append(({"band": 1 - band}, band == 0, band == 1, None, ("border", 1 - band), band == 0))
    elif band_count > 2:
        found.append(({"band": band - 1}, None, band > 0, band < band_count - 1, ("border", 0), band < band_count - 1))
        found.append(({"band": band + 1}, band < band_count - 1, None, band > 0, ("border", 1), None))
    if slab_count > 1:
        found.append(({"tm": slab + 1}, slab < slab_count - 1, None, slab > 0, ("adj", 0), None))
    return found


def when(condition):
    return (lambda body: body()) if condition is None else pl.when(condition)


def value_chunks(heads):
    return [(0, (heads - 1) * BLK), ((heads - 1) * BLK, BLK)]


def ahead_parts(heads):
    return [(0, BLK)]


def weigh(query, key):
    scores = lax.dot_general(
        query, key, (((1,), (1,)), ((), ())), preferred_element_type=jnp.float32
    )
    return scores * SCALE2


def kernel(
    clip_count, slab_count, band_count, q_hbm, k_hbm, v_hbm, adj_hbm, border_hbm, out_ref,
    q_ref, k_ref, v_ref, adj_ref, border_ref, send_ref, recv_ref, acc_ref, weights_ref, share_ref,
    both_ref, pass_ref, peer_adj_ref, peer_border_ref,
    load_sem, here_sem, send_sem, recv_sem, ahead_send_sem, ahead_recv_sem, pass_send_sem, pass_recv_sem,
    relay_send_sem, relay_recv_sem,
):
    plan = routes(slab_count, band_count)
    slots = range(len(plan))
    rows, width = q_ref.shape
    heads = width // HD
    late = lax.axis_index("head") > 0
    early = jnp.logical_not(late)

    neighbours = []
    for axis, count in (("tm", slab_count), ("band", band_count), ("clip", clip_count)):
        if count > 1:
            index = lax.axis_index(axis)
            lower, upper = index > 0, index < count - 1
            if axis == "clip":
                lower, upper = lower & late, upper & late
            neighbours.append((axis, index, lower, upper))
    others = sum(axis != "clip" for axis, *_ in neighbours)

    detours = {}
    if clip_count > 1 and slab_count > 1 and band_count > 1:
        for slot, (_, _, _, _, (kind, _), above) in enumerate(plan):
            if above is not None:
                detours[slot] = ROUTE_X if kind == "border" else ROUTE_Z

    def at(clip, slab, band):
        place = [lax.axis_index(axis) for axis in ("clip", "tm", "band")]
        return (place[0] == clip) & (place[1] == slab) & (place[2] == band) & late

    lends = {slot: at(*source) for slot, (source, _) in detours.items()}
    relays = {slot: at(*middle) for slot, (_, middle) in detours.items()}
    corner = at(0, 0, 0)

    def lend(slot):
        return pltpu.make_async_remote_copy(
            src_ref=send_ref.at[slot, 1, pl.ds(0, BLK)],
            dst_ref=pass_ref.at[slot],
            send_sem=pass_send_sem.at[slot],
            recv_sem=pass_recv_sem.at[slot],
            device_id=dict(zip(("clip", "tm", "band"), detours[slot][1])),
            device_id_type=MESH,
        )

    def relay(slot):
        return pltpu.make_async_remote_copy(
            src_ref=pass_ref.at[slot],
            dst_ref=recv_ref.at[slot, 1, pl.ds(0, BLK)],
            send_sem=relay_send_sem.at[slot],
            recv_sem=relay_recv_sem.at[slot],
            device_id={"clip": 0, "tm": 0, "band": 0},
            device_id_type=MESH,
        )

    barrier = pltpu.get_barrier_semaphore()
    for axis, index, _, has_upper in neighbours:
        @pl.when(has_upper)
        def _():
            pl.semaphore_signal(barrier, inc=1, device_id={axis: index + 1}, device_id_type=MESH)

    loads = [
        pltpu.make_async_copy(source, target, load_sem.at[number])
        for number, (source, target) in enumerate(
            ((k_hbm, k_ref), (adj_hbm, adj_ref), (border_hbm, border_ref), (v_hbm, v_ref), (q_hbm, q_ref))
        )
    ]
    for load in loads[:3]:
        load.start()

    chunks = [[(0, heads * BLK)], value_chunks(heads)]
    pieces_ahead = ahead_parts(heads)
    skipped = sum(size for _, size in pieces_ahead)

    def transfer(slot, part, group, skip=0):
        start, size = chunks[part][group]
        at = (slot, part, pl.ds(start + skip, size - skip))
        return pltpu.make_async_remote_copy(
            src_ref=send_ref.at[at],
            dst_ref=recv_ref.at[at],
            send_sem=send_sem.at[slot, part, group],
            recv_sem=recv_sem.at[slot, part, group],
            device_id=plan[slot][0],
            device_id_type=MESH,
        )

    def ahead(slot):
        mask = (adj_hbm, peer_adj_ref) if plan[slot][4][0] == "adj" else (border_hbm, peer_border_ref)
        parts = [
            (k_hbm.at[:, pl.ds(0, size), pl.ds(head * HD, HD)], both_ref.at[slot, head, :, pl.ds(0, size)])
            for head, size in pieces_ahead
        ]
        return [
            pltpu.make_async_remote_copy(
                src_ref=source,
                dst_ref=target,
                send_sem=ahead_send_sem.at[slot, number],
                recv_sem=ahead_recv_sem.at[slot, number],
                device_id=plan[slot][0],
                device_id_type=MESH,
            )
            for number, (source, target) in enumerate(parts + [mask])
        ]

    def send(slot, part, downward):
        _, up, down, _, _, above = plan[slot]
        sends = down if downward else up
        if sends is None:
            return
        for group in range(len(chunks[part])):
            short, skip = late, skipped
            if part:
                short, skip = lends.get(slot), BLK
            if downward and group == 0 and above is not None and short is not None:
                @pl.when(sends & short)
                def _():
                    transfer(slot, part, group, skip).start()

                @pl.when(sends & jnp.logical_not(short))
                def _():
                    transfer(slot, part, group).start()
            else:
                @pl.when(sends)
                def _():
                    transfer(slot, part, group).start()

    arrivals = sum(lower.astype(jnp.int32) for _, _, lower, _ in neighbours)

    @pl.when(arrivals > 0)
    def _():
        pl.semaphore_wait(barrier, arrivals)

    for slot, (_, _, down, _, _, above) in enumerate(plan):
        if above is not None:
            @pl.when(down & late)
            def _():
                for copy in ahead(slot):
                    copy.start()

    for number, (axis, index, has_lower, _) in enumerate(neighbours):
        @pl.when(has_lower)
        def _():
            pl.semaphore_signal(
                here_sem.at[number], inc=1, device_id={axis: index - 1}, device_id_type=MESH
            )

    for load in loads[3:]:
        load.start()
    for load in loads[1:3]:
        load.wait()
    blocks = [
        adj_ref[row, 1] if kind == "adj" else border_ref[0, row] for _, _, _, _, (kind, row), _ in plan
    ]

    def pick(slot, part, whole):
        for head in range(heads):
            send_ref[slot, part, head * BLK : (head + 1) * BLK] = whole[
                blocks[slot], :, head * HD : (head + 1) * HD
            ]

    loads[0].wait()
    for slot in slots:
        pick(slot, 0, k_ref)
        send(slot, 0, True)
    for number, (_, _, _, has_upper) in enumerate(neighbours[:others]):
        @pl.when(has_upper)
        def _():
            pl.semaphore_wait(here_sem.at[number], 1)
    for slot in slots:
        send(slot, 0, False)

    loads[3].wait()
    for slot in slots:
        pick(slot, 1, v_ref)
    if clip_count > 1:
        @pl.when(neighbours[others][3])
        def _():
            pl.semaphore_wait(here_sem.at[others], 1)
    for slot in detours:
        @pl.when(lends[slot])
        def _():
            lend(slot).start()

    def send_values():
        for slot in slots:
            send(slot, 1, True)
            send(slot, 1, False)

    pl.when(early)(send_values)

    for slot, (_, _, _, comes, _, _) in enumerate(plan):
        if comes is not None:
            @pl.when(jnp.logical_not(comes))
            def _():
                recv_ref[slot] = jnp.zeros(recv_ref.shape[1:], recv_ref.dtype)

    loads[4].wait()
    own = []
    for head in range(heads):
        columns = slice(head * HD, (head + 1) * HD)
        scores = weigh(q_ref[:, columns], k_ref[:, :, columns].reshape(rows, HD))
        most = jnp.max(scores, axis=1, keepdims=True)
        weights = jnp.exp2(scores - most)
        total = jnp.sum(weights, axis=1, keepdims=True)
        acc_ref[head] = jnp.dot(
            weights.astype(jnp.bfloat16), v_ref[:, :, columns].reshape(rows, HD), preferred_element_type=jnp.float32
        )
        own.append((most, total))

    for slot, (*_, above) in enumerate(plan):
        if above is not None:
            @pl.when(above & late)
            def _():
                for copy in ahead(slot):
                    copy.wait_recv()

    for slot, (_, _, _, comes, (kind, _), above) in enumerate(plan):
        if above is None:
            @when(comes)
            def _():
                transfer(slot, 0, 0).wait_recv()
        else:
            @pl.when(above & late)
            def _():
                block = peer_adj_ref[1, 1] if kind == "adj" else peer_border_ref[0, 0]
                for head, size in pieces_ahead:
                    recv_ref[slot, 0, head * BLK : head * BLK + size] = both_ref[slot, head, block, :size]
                transfer(slot, 0, 0, skipped).wait_recv()

            whole = jnp.logical_not(above & late)

            @pl.when(whole if comes is None else whole & comes)
            def _():
                transfer(slot, 0, 0).wait_recv()

    for slot in detours:
        @pl.when(relays[slot])
        def _():
            lend(slot).wait_recv()
            relay(slot).start()

    pl.when(late)(send_values)

    def arrived(part, head):
        return jnp.concatenate(
            [recv_ref[slot, part, head * BLK : (head + 1) * BLK] for slot in slots], axis=0
        )

    hidden = [
        None if comes is None else jnp.where(comes, 0.0, masked_score).astype(jnp.float32)
        for _, _, _, comes, _, _ in plan
    ]
    for head in range(heads):
        columns = slice(head * HD, (head + 1) * HD)
        scores = weigh(q_ref[:, columns], arrived(0, head))
        scores = [
            scores[:, slot * BLK : (slot + 1) * BLK] + (0.0 if hidden[slot] is None else hidden[slot]) for slot in slots
        ]
        most, total = own[head]
        largest = jnp.maximum(
            most, jnp.max(functools.reduce(jnp.maximum, scores), axis=1, keepdims=True)
        )
        weights = [jnp.exp2(score - largest) for score in scores]
        factor = jnp.exp2(most - largest)
        share = 1.0 / (factor * total + jnp.sum(sum(weights), axis=1, keepdims=True))
        acc_ref[head] = acc_ref[head] * factor
        share_ref[head] = jnp.broadcast_to(share, (rows, HD))
        for slot in slots:
            weights_ref[head, :, slot * BLK : (slot + 1) * BLK] = weights[slot].astype(jnp.bfloat16)

    for group, (start, size) in enumerate(chunks[1]):
        for slot, (_, _, _, comes, _, _) in enumerate(plan):
            if slot in detours and group == 0:
                @pl.when(corner)
                def _():
                    relay(slot).wait_recv()
                    transfer(slot, 1, group, BLK).wait_recv()

                whole = jnp.logical_not(corner)

                @pl.when(whole if comes is None else whole & comes)
                def _():
                    transfer(slot, 1, group).wait_recv()
            else:
                @when(comes)
                def _():
                    transfer(slot, 1, group).wait_recv()
        for head in range(start // BLK, (start + size) // BLK):
            result = acc_ref[head] + jnp.dot(
                weights_ref[head], arrived(1, head), preferred_element_type=jnp.float32
            )
            out_ref[:, head * HD : (head + 1) * HD] = (result * share_ref[head]).astype(out_ref.dtype)

    for slot, (_, up, down, _, _, above) in enumerate(plan):
        sends = down if up is None else up if down is None else None
        if above is None:
            @when(sends)
            def _():
                transfer(slot, 0, 0).wait_send()
        else:
            @pl.when(down & late)
            def _():
                for copy in ahead(slot):
                    copy.wait_send()
                transfer(slot, 0, 0, skipped).wait_send()

            whole = jnp.logical_not(down & late)

            @pl.when(whole if sends is None else whole & sends)
            def _():
                transfer(slot, 0, 0).wait_send()
        for group in range(len(chunks[1])):
            if slot in detours and group == 0:
                @pl.when(lends[slot])
                def _():
                    lend(slot).wait_send()
                    transfer(slot, 1, group, BLK).wait_send()

                @pl.when(relays[slot])
                def _():
                    relay(slot).wait_send()

                whole = jnp.logical_not(lends[slot])

                @pl.when(whole if sends is None else whole & sends)
                def _():
                    transfer(slot, 1, group).wait_send()
            else:
                @when(sends)
                def _():
                    transfer(slot, 1, group).wait_send()


def per_device(queries, keys, values, adj_mask, border_blocks):
    rows, width = queries.shape[2:]
    heads = width // HD
    clip_count, slab_count, band_count = (lax.axis_size(axis) for axis in ("clip", "tm", "band"))
    sources = (2 if slab_count > 1 else 0) + min(band_count - 1, 2)
    assert rows == 2 * BLK and adj_mask.shape[3] == 2 and border_blocks.shape[3] == 1
    pieces = len(ahead_parts(heads))
    block_sems = pltpu.SemaphoreType.DMA((sources, 2, len(value_chunks(heads))))
    ahead_sems = pltpu.SemaphoreType.DMA((sources, pieces + 1))
    attended = pl.pallas_call(
        functools.partial(kernel, clip_count, slab_count, band_count),
        out_shape=pltpu.VMEM((rows, width), jnp.bfloat16),
        in_specs=[pl.BlockSpec(memory_space=pl.ANY)] * 5,
        out_specs=pl.BlockSpec(memory_space=pltpu.VMEM),
        scratch_shapes=[
            pltpu.VMEM((rows, width), jnp.bfloat16),
            pltpu.VMEM((rows // BLK, BLK, width), jnp.bfloat16),
            pltpu.VMEM((rows // BLK, BLK, width), jnp.bfloat16),
            pltpu.SMEM(adj_mask.shape[2:], jnp.int32),
            pltpu.SMEM(border_blocks.shape[:1:-1], jnp.int32),
            pltpu.VMEM((sources, 2, heads * BLK, HD), jnp.bfloat16),
            pltpu.VMEM((sources, 2, heads * BLK, HD), jnp.bfloat16),
            pltpu.VMEM((heads, rows, HD), jnp.float32),
            pltpu.VMEM((heads, rows, sources * BLK), jnp.bfloat16),
            pltpu.VMEM((heads, rows, HD), jnp.float32),
            pltpu.VMEM((sources, pieces, rows // BLK, BLK, HD), jnp.bfloat16),
            pltpu.VMEM((sources, BLK, HD), jnp.bfloat16),
            pltpu.SMEM(adj_mask.shape[2:], jnp.int32),
            pltpu.SMEM(border_blocks.shape[:1:-1], jnp.int32),
            pltpu.SemaphoreType.DMA((5,)),
            pltpu.SemaphoreType.REGULAR((max(1, (slab_count > 1) + (band_count > 1) + (clip_count > 1)),)),
            block_sems,
            block_sems,
            ahead_sems,
            ahead_sems,
            pltpu.SemaphoreType.DMA((sources,)),
            pltpu.SemaphoreType.DMA((sources,)),
            pltpu.SemaphoreType.DMA((sources,)),
            pltpu.SemaphoreType.DMA((sources,)),
        ],
        compiler_params=pltpu.CompilerParams(collective_id=0, has_side_effects=True),
        name="radial_attention",
    )(
        queries[0, 0],
        keys.reshape(rows // BLK, BLK, width),
        values.reshape(rows // BLK, BLK, width),
        adj_mask[0, 0], border_blocks[0, 0].T,
    )
    return attended[None, None]


def solution(mesh):
    placed = (
        P(("clip", "tm"), "band", None, "head"),
        P(("clip", "tm"), "band", None, "head"),
        P(("clip", "tm"), "band", None, "head"),
        P(("clip", "tm"), "band", None, None),
        P(("clip", "tm"), "band", None, None),
    )
    return jax.shard_map(
        per_device,
        mesh=mesh,
        in_specs=placed,
        out_specs=P(("clip", "tm"), "band", None, "head"),
        check_vma=False,
    )
```

```python
import functools
import math

import jax
import jax.numpy as jnp
from jax import lax
from jax.experimental import pallas as pl
from jax.experimental.pallas import tpu as pltpu
from jax.sharding import PartitionSpec as P

BLK = 128
HD = 128

masked_score = -1e30
SCALE2 = math.log2(math.e) / math.sqrt(HD)
MESH = pl.DeviceIdType.MESH
TAIL = 1

ROUTE_X = ((0, 0, 1), (1, 0, 1))
ROUTE_Z = ((0, 1, 0), (1, 1, 0))


def routes(slab_count, band_count):
    slab, band = lax.axis_index("tm"), lax.axis_index("band")
    found = []
    if slab_count > 1:
        found.append(({"tm": slab - 1}, None, slab > 0, slab < slab_count - 1, ("adj", 1), slab < slab_count - 1))
    if band_count == 2:
        found.append(({"band": 1 - band}, band == 0, band == 1, None, ("border", 1 - band), band == 0))
    elif band_count > 2:
        found.append(({"band": band - 1}, None, band > 0, band < band_count - 1, ("border", 0), band < band_count - 1))
        found.append(({"band": band + 1}, band < band_count - 1, None, band > 0, ("border", 1), None))
    if slab_count > 1:
        found.append(({"tm": slab + 1}, slab < slab_count - 1, None, slab > 0, ("adj", 0), None))
    return found


def when(condition):
    return (lambda body: body()) if condition is None else pl.when(condition)


def last_heads(heads):
    return TAIL if heads > 2 * TAIL else 1


def value_chunks(heads):
    most = heads - last_heads(heads)
    return [(0, most * BLK), (most * BLK, (heads - most) * BLK)]


def ahead_parts(heads):
    return [(0, BLK)]


def weigh(query, key):
    scores = lax.dot_general(
        query, key, (((1,), (1,)), ((), ())), preferred_element_type=jnp.float32
    )
    return scores * SCALE2


def kernel(
    clip_count, slab_count, band_count, q_hbm, k_hbm, v_hbm, adj_hbm, border_hbm,
    out_ref, last_acc_ref, last_weights_ref, last_share_ref, last_recv_ref,
    q_ref, k_ref, v_ref, adj_ref, border_ref, send_ref, recv_ref, acc_ref, weights_ref, share_ref,
    both_ref, pass_ref, peer_adj_ref, peer_border_ref,
    load_sem, here_sem, send_sem, recv_sem, ahead_send_sem, ahead_recv_sem, pass_send_sem, pass_recv_sem,
    relay_send_sem, relay_recv_sem,
):
    plan = routes(slab_count, band_count)
    slots = range(len(plan))
    rows, width = q_ref.shape
    heads = width // HD
    late = lax.axis_index("head") > 0
    early = jnp.logical_not(late)

    neighbours = []
    for axis, count in (("tm", slab_count), ("band", band_count), ("clip", clip_count)):
        if count > 1:
            index = lax.axis_index(axis)
            lower, upper = index > 0, index < count - 1
            if axis == "clip":
                lower, upper = lower & late, upper & late
            neighbours.append((axis, index, lower, upper))
    others = sum(axis != "clip" for axis, *_ in neighbours)

    detours = {}
    if clip_count > 1 and slab_count > 1 and band_count > 1:
        for slot, (_, _, _, _, (kind, _), above) in enumerate(plan):
            if above is not None:
                detours[slot] = ROUTE_X if kind == "border" else ROUTE_Z

    def at(clip, slab, band):
        place = [lax.axis_index(axis) for axis in ("clip", "tm", "band")]
        return (place[0] == clip) & (place[1] == slab) & (place[2] == band) & late

    lends = {slot: at(*source) for slot, (source, _) in detours.items()}
    relays = {slot: at(*middle) for slot, (_, middle) in detours.items()}
    corner = at(0, 0, 0)

    def lend(slot):
        return pltpu.make_async_remote_copy(
            src_ref=send_ref.at[slot, 1, pl.ds(0, BLK)],
            dst_ref=pass_ref.at[slot],
            send_sem=pass_send_sem.at[slot],
            recv_sem=pass_recv_sem.at[slot],
            device_id=dict(zip(("clip", "tm", "band"), detours[slot][1])),
            device_id_type=MESH,
        )

    def relay(slot):
        return pltpu.make_async_remote_copy(
            src_ref=pass_ref.at[slot],
            dst_ref=recv_ref.at[slot, 1, pl.ds(0, BLK)],
            send_sem=relay_send_sem.at[slot],
            recv_sem=relay_recv_sem.at[slot],
            device_id={"clip": 0, "tm": 0, "band": 0},
            device_id_type=MESH,
        )

    barrier = pltpu.get_barrier_semaphore()
    for axis, index, _, has_upper in neighbours:
        @pl.when(has_upper)
        def _():
            pl.semaphore_signal(barrier, inc=1, device_id={axis: index + 1}, device_id_type=MESH)

    loads = [
        pltpu.make_async_copy(source, target, load_sem.at[number])
        for number, (source, target) in enumerate(
            ((k_hbm, k_ref), (adj_hbm, adj_ref), (border_hbm, border_ref), (v_hbm, v_ref), (q_hbm, q_ref))
        )
    ]
    for load in loads[:3]:
        load.start()

    chunks = [[(0, heads * BLK)], value_chunks(heads)]
    pieces_ahead = ahead_parts(heads)
    skipped = sum(size for _, size in pieces_ahead)

    def transfer(slot, part, group, skip=0):
        start, size = chunks[part][group]
        at = (slot, part, pl.ds(start + skip, size - skip))
        return pltpu.make_async_remote_copy(
            src_ref=send_ref.at[at],
            dst_ref=last_recv_ref.at[slot] if group else recv_ref.at[at],
            send_sem=send_sem.at[slot, part, group],
            recv_sem=recv_sem.at[slot, part, group],
            device_id=plan[slot][0],
            device_id_type=MESH,
        )

    def ahead(slot):
        mask = (adj_hbm, peer_adj_ref) if plan[slot][4][0] == "adj" else (border_hbm, peer_border_ref)
        parts = [
            (k_hbm.at[:, pl.ds(0, size), pl.ds(head * HD, HD)], both_ref.at[slot, head, :, pl.ds(0, size)])
            for head, size in pieces_ahead
        ]
        return [
            pltpu.make_async_remote_copy(
                src_ref=source,
                dst_ref=target,
                send_sem=ahead_send_sem.at[slot, number],
                recv_sem=ahead_recv_sem.at[slot, number],
                device_id=plan[slot][0],
                device_id_type=MESH,
            )
            for number, (source, target) in enumerate(parts + [mask])
        ]

    def send(slot, part, downward):
        _, up, down, _, _, above = plan[slot]
        sends = down if downward else up
        if sends is None:
            return
        for group in range(len(chunks[part])):
            short, skip = late, skipped
            if part:
                short, skip = lends.get(slot), BLK
            if downward and group == 0 and above is not None and short is not None:
                @pl.when(sends & short)
                def _():
                    transfer(slot, part, group, skip).start()

                @pl.when(sends & jnp.logical_not(short))
                def _():
                    transfer(slot, part, group).start()
            else:
                @pl.when(sends)
                def _():
                    transfer(slot, part, group).start()

    arrivals = sum(lower.astype(jnp.int32) for _, _, lower, _ in neighbours)

    @pl.when(arrivals > 0)
    def _():
        pl.semaphore_wait(barrier, arrivals)

    for slot, (_, _, down, _, _, above) in enumerate(plan):
        if above is not None:
            @pl.when(down & late)
            def _():
                for copy in ahead(slot):
                    copy.start()

    for number, (axis, index, has_lower, _) in enumerate(neighbours):
        @pl.when(has_lower)
        def _():
            pl.semaphore_signal(
                here_sem.at[number], inc=1, device_id={axis: index - 1}, device_id_type=MESH
            )

    for load in loads[3:]:
        load.start()
    for load in loads[1:3]:
        load.wait()
    blocks = [
        adj_ref[row, 1] if kind == "adj" else border_ref[0, row] for _, _, _, _, (kind, row), _ in plan
    ]

    def pick(slot, part, whole):
        for head in range(heads):
            send_ref[slot, part, head * BLK : (head + 1) * BLK] = whole[
                blocks[slot], :, head * HD : (head + 1) * HD
            ]

    loads[0].wait()
    for slot in slots:
        pick(slot, 0, k_ref)
        send(slot, 0, True)
    for number, (_, _, _, has_upper) in enumerate(neighbours[:others]):
        @pl.when(has_upper)
        def _():
            pl.semaphore_wait(here_sem.at[number], 1)
    for slot in slots:
        send(slot, 0, False)

    loads[3].wait()
    for slot in slots:
        pick(slot, 1, v_ref)
    if clip_count > 1:
        @pl.when(neighbours[others][3])
        def _():
            pl.semaphore_wait(here_sem.at[others], 1)
    for slot in detours:
        @pl.when(lends[slot])
        def _():
            lend(slot).start()

    def send_values():
        for slot in slots:
            send(slot, 1, True)
            send(slot, 1, False)

    pl.when(early)(send_values)

    for slot, (_, _, _, comes, _, _) in enumerate(plan):
        if comes is not None:
            @pl.when(jnp.logical_not(comes))
            def _():
                recv_ref[slot] = jnp.zeros(recv_ref.shape[1:], recv_ref.dtype)
                last_recv_ref[slot] = jnp.zeros(last_recv_ref.shape[1:], recv_ref.dtype)

    first_last = heads - last_acc_ref.shape[0]

    def kept(head):
        if head < first_last:
            return acc_ref.at[head], weights_ref.at[head], share_ref.at[head]
        number = head - first_last
        return last_acc_ref.at[number], last_weights_ref.at[number], last_share_ref.at[number]

    loads[4].wait()
    own = []
    for head in range(heads):
        columns = slice(head * HD, (head + 1) * HD)
        scores = weigh(q_ref[:, columns], k_ref[:, :, columns].reshape(rows, HD))
        most = jnp.max(scores, axis=1, keepdims=True)
        weights = jnp.exp2(scores - most)
        total = jnp.sum(weights, axis=1, keepdims=True)
        kept(head)[0][...] = jnp.dot(
            weights.astype(jnp.bfloat16), v_ref[:, :, columns].reshape(rows, HD), preferred_element_type=jnp.float32
        )
        own.append((most, total))

    for slot, (*_, above) in enumerate(plan):
        if above is not None:
            @pl.when(above & late)
            def _():
                for copy in ahead(slot):
                    copy.wait_recv()

    for slot, (_, _, _, comes, (kind, _), above) in enumerate(plan):
        if above is None:
            @when(comes)
            def _():
                transfer(slot, 0, 0).wait_recv()
        else:
            @pl.when(above & late)
            def _():
                block = peer_adj_ref[1, 1] if kind == "adj" else peer_border_ref[0, 0]
                for head, size in pieces_ahead:
                    recv_ref[slot, 0, head * BLK : head * BLK + size] = both_ref[slot, head, block, :size]
                transfer(slot, 0, 0, skipped).wait_recv()

            whole = jnp.logical_not(above & late)

            @pl.when(whole if comes is None else whole & comes)
            def _():
                transfer(slot, 0, 0).wait_recv()

    for slot in detours:
        @pl.when(relays[slot])
        def _():
            lend(slot).wait_recv()
            relay(slot).start()

    pl.when(late)(send_values)

    def arrived(part, head):
        return jnp.concatenate(
            [recv_ref[slot, part, head * BLK : (head + 1) * BLK] for slot in slots], axis=0
        )

    hidden = [
        None if comes is None else jnp.where(comes, 0.0, masked_score).astype(jnp.float32)
        for _, _, _, comes, _, _ in plan
    ]
    for head in range(heads):
        columns = slice(head * HD, (head + 1) * HD)
        scores = weigh(q_ref[:, columns], arrived(0, head))
        scores = [
            scores[:, slot * BLK : (slot + 1) * BLK] + (0.0 if hidden[slot] is None else hidden[slot]) for slot in slots
        ]
        most, total = own[head]
        largest = jnp.maximum(
            most, jnp.max(functools.reduce(jnp.maximum, scores), axis=1, keepdims=True)
        )
        weights = [jnp.exp2(score - largest) for score in scores]
        factor = jnp.exp2(most - largest)
        share = 1.0 / (factor * total + jnp.sum(sum(weights), axis=1, keepdims=True))
        sum_ref, part_ref, scale_ref = kept(head)
        sum_ref[...] = sum_ref[...] * factor
        scale_ref[...] = jnp.broadcast_to(share, (rows, HD))
        for slot in slots:
            part_ref[:, slot * BLK : (slot + 1) * BLK] = weights[slot].astype(jnp.bfloat16)

    for group, (start, size) in enumerate(chunks[1]):
        for slot, (_, _, _, comes, _, _) in enumerate(plan):
            if slot in detours and group == 0:
                @pl.when(corner)
                def _():
                    relay(slot).wait_recv()
                    transfer(slot, 1, group, BLK).wait_recv()

                whole = jnp.logical_not(corner)

                @pl.when(whole if comes is None else whole & comes)
                def _():
                    transfer(slot, 1, group).wait_recv()
            else:
                @when(comes)
                def _():
                    transfer(slot, 1, group).wait_recv()
        for head in range(start // BLK, min((start + size) // BLK, first_last)):
            result = acc_ref[head] + jnp.dot(
                weights_ref[head], arrived(1, head), preferred_element_type=jnp.float32
            )
            out_ref[:, head * HD : (head + 1) * HD] = (result * share_ref[head]).astype(out_ref.dtype)

    for slot, (_, up, down, _, _, above) in enumerate(plan):
        sends = down if up is None else up if down is None else None
        if above is None:
            @when(sends)
            def _():
                transfer(slot, 0, 0).wait_send()
        else:
            @pl.when(down & late)
            def _():
                for copy in ahead(slot):
                    copy.wait_send()
                transfer(slot, 0, 0, skipped).wait_send()

            whole = jnp.logical_not(down & late)

            @pl.when(whole if sends is None else whole & sends)
            def _():
                transfer(slot, 0, 0).wait_send()
        for group in range(len(chunks[1])):
            if slot in detours and group == 0:
                @pl.when(lends[slot])
                def _():
                    lend(slot).wait_send()
                    transfer(slot, 1, group, BLK).wait_send()

                @pl.when(relays[slot])
                def _():
                    relay(slot).wait_send()

                whole = jnp.logical_not(lends[slot])

                @pl.when(whole if sends is None else whole & sends)
                def _():
                    transfer(slot, 1, group).wait_send()
            else:
                @when(sends)
                def _():
                    transfer(slot, 1, group).wait_send()


def finish(done_ref, acc_ref, weights_ref, share_ref, recv_ref, out_hbm, last_ref, sem):
    width = done_ref.shape[1]
    copies = [
        pltpu.make_async_copy(done_ref, out_hbm.at[:, pl.ds(0, width)], sem.at[0]),
        pltpu.make_async_copy(last_ref, out_hbm.at[:, pl.ds(width, last_ref.shape[1])], sem.at[1]),
    ]
    copies[0].start()
    for head in range(acc_ref.shape[0]):
        values = jnp.concatenate(
            [recv_ref[slot, head * BLK : (head + 1) * BLK] for slot in range(recv_ref.shape[0])], axis=0
        )
        result = acc_ref[head] + jnp.dot(weights_ref[head], values, preferred_element_type=jnp.float32)
        last_ref[:, head * HD : (head + 1) * HD] = (result * share_ref[head]).astype(last_ref.dtype)
    copies[1].start()
    for copy in copies:
        copy.wait()


def per_device(queries, keys, values, adj_mask, border_blocks):
    rows, width = queries.shape[2:]
    heads = width // HD
    clip_count, slab_count, band_count = (lax.axis_size(axis) for axis in ("clip", "tm", "band"))
    sources = (2 if slab_count > 1 else 0) + min(band_count - 1, 2)
    assert rows == 2 * BLK and adj_mask.shape[3] == 2 and border_blocks.shape[3] == 1
    pieces = len(ahead_parts(heads))
    block_sems = pltpu.SemaphoreType.DMA((sources, 2, len(value_chunks(heads))))
    ahead_sems = pltpu.SemaphoreType.DMA((sources, pieces + 1))
    last = last_heads(heads)
    parts = pl.pallas_call(
        functools.partial(kernel, clip_count, slab_count, band_count),
        out_shape=[
            pltpu.VMEM((rows, width - last * HD), jnp.bfloat16),
            pltpu.VMEM((last, rows, HD), jnp.float32),
            pltpu.VMEM((last, rows, sources * BLK), jnp.bfloat16),
            pltpu.VMEM((last, rows, HD), jnp.float32),
            pltpu.VMEM((sources, last * BLK, HD), jnp.bfloat16),
        ],
        in_specs=[pl.BlockSpec(memory_space=pl.ANY)] * 5,
        out_specs=[pl.BlockSpec(memory_space=pltpu.VMEM)] * 5,
        scratch_shapes=[
            pltpu.VMEM((rows, width), jnp.bfloat16),
            pltpu.VMEM((rows // BLK, BLK, width), jnp.bfloat16),
            pltpu.VMEM((rows // BLK, BLK, width), jnp.bfloat16),
            pltpu.SMEM(adj_mask.shape[2:], jnp.int32),
            pltpu.SMEM(border_blocks.shape[:1:-1], jnp.int32),
            pltpu.VMEM((sources, 2, heads * BLK, HD), jnp.bfloat16),
            pltpu.VMEM((sources, 2, heads * BLK, HD), jnp.bfloat16),
            pltpu.VMEM((heads, rows, HD), jnp.float32),
            pltpu.VMEM((heads, rows, sources * BLK), jnp.bfloat16),
            pltpu.VMEM((heads, rows, HD), jnp.float32),
            pltpu.VMEM((sources, pieces, rows // BLK, BLK, HD), jnp.bfloat16),
            pltpu.VMEM((sources, BLK, HD), jnp.bfloat16),
            pltpu.SMEM(adj_mask.shape[2:], jnp.int32),
            pltpu.SMEM(border_blocks.shape[:1:-1], jnp.int32),
            pltpu.SemaphoreType.DMA((5,)),
            pltpu.SemaphoreType.REGULAR((max(1, (slab_count > 1) + (band_count > 1) + (clip_count > 1)),)),
            block_sems,
            block_sems,
            ahead_sems,
            ahead_sems,
            pltpu.SemaphoreType.DMA((sources,)),
            pltpu.SemaphoreType.DMA((sources,)),
            pltpu.SemaphoreType.DMA((sources,)),
            pltpu.SemaphoreType.DMA((sources,)),
        ],
        compiler_params=pltpu.CompilerParams(collective_id=0, has_side_effects=True),
        name="radial_attention",
    )(
        queries[0, 0],
        keys.reshape(rows // BLK, BLK, width),
        values.reshape(rows // BLK, BLK, width),
        adj_mask[0, 0], border_blocks[0, 0].T,
    )
    attended = pl.pallas_call(
        finish,
        out_shape=jax.ShapeDtypeStruct((rows, width), jnp.bfloat16),
        in_specs=[pl.BlockSpec(memory_space=pltpu.VMEM)] * 5,
        out_specs=pl.BlockSpec(memory_space=pl.ANY),
        scratch_shapes=[pltpu.VMEM((rows, last * HD), jnp.bfloat16), pltpu.SemaphoreType.DMA((2,))],
        name="last_heads",
    )(*(pltpu.with_memory_space_constraint(part, pltpu.VMEM) for part in parts))
    return attended[None, None]


def solution(mesh):
    placed = (
        P(("clip", "tm"), "band", None, "head"),
        P(("clip", "tm"), "band", None, "head"),
        P(("clip", "tm"), "band", None, "head"),
        P(("clip", "tm"), "band", None, None),
        P(("clip", "tm"), "band", None, None),
    )
    return jax.shard_map(
        per_device,
        mesh=mesh,
        in_specs=placed,
        out_specs=P(("clip", "tm"), "band", None, "head"),
        check_vma=False,
    )
```

```python
import functools
import math

import jax
import jax.numpy as jnp
from jax import lax
from jax.experimental import pallas as pl
from jax.experimental.pallas import tpu as pltpu
from jax.sharding import PartitionSpec as P

BLK = 128
HD = 128

masked_score = -1e30
SCALE2 = math.log2(math.e) / math.sqrt(HD)
MESH = pl.DeviceIdType.MESH
TAIL = 1

ROUTE_X = ((0, 0, 1), (1, 0, 1))
ROUTE_Z = ((0, 1, 0), (1, 1, 0))


def routes(slab_count, band_count):
    slab, band = lax.axis_index("tm"), lax.axis_index("band")
    found = []
    if slab_count > 1:
        found.append(({"tm": slab - 1}, None, slab > 0, slab < slab_count - 1, ("adj", 1), slab < slab_count - 1))
    if band_count == 2:
        found.append(({"band": 1 - band}, band == 0, band == 1, None, ("border", 1 - band), band == 0))
    elif band_count > 2:
        found.append(({"band": band - 1}, None, band > 0, band < band_count - 1, ("border", 0), band < band_count - 1))
        found.append(({"band": band + 1}, band < band_count - 1, None, band > 0, ("border", 1), None))
    if slab_count > 1:
        found.append(({"tm": slab + 1}, slab < slab_count - 1, None, slab > 0, ("adj", 0), None))
    return found


def when(condition):
    return (lambda body: body()) if condition is None else pl.when(condition)


def last_heads(heads):
    return TAIL if heads > 2 * TAIL else 1


def value_chunks(heads):
    most = heads - last_heads(heads)
    return [(0, most * BLK), (most * BLK, (heads - most) * BLK)]


FLAG = 16


def weigh(query, key):
    scores = lax.dot_general(
        query, key, (((1,), (1,)), ((), ())), preferred_element_type=jnp.float32
    )
    return scores * SCALE2


def kernel(
    clip_count, slab_count, band_count, q_hbm, k_hbm, v_hbm, adj_hbm, border_hbm,
    out_ref, last_acc_ref, last_weights_ref, last_share_ref, last_recv_ref,
    vq_ref, k_ref, adj_ref, border_ref, send_ref, recv_ref, acc_ref, weights_ref, share_ref,
    both_ref, pass_ref,
    load_sem, here_sem, send_sem, ahead_sem, pass_sem, key_sem, value_sem,
):
    plan = routes(slab_count, band_count)
    slots = range(len(plan))
    rows, width = k_ref.shape[0] * BLK, k_ref.shape[2]
    heads = width // HD
    late = lax.axis_index("head") > 0
    early = jnp.logical_not(late)

    neighbours = []
    for axis, count in (("tm", slab_count), ("band", band_count), ("clip", clip_count)):
        if count > 1:
            index = lax.axis_index(axis)
            lower, upper = index > 0, index < count - 1
            if axis == "clip":
                lower, upper = lower & late, upper & late
            neighbours.append((axis, index, lower, upper))

    detours = {}
    if clip_count > 1 and slab_count > 1 and band_count > 1:
        for slot, (_, _, _, _, (kind, _), above) in enumerate(plan):
            if above is not None:
                detours[slot] = ROUTE_X if kind == "border" else ROUTE_Z

    def at(clip, slab, band):
        place = [lax.axis_index(axis) for axis in ("clip", "tm", "band")]
        return (place[0] == clip) & (place[1] == slab) & (place[2] == band) & late

    lends = {slot: at(*source) for slot, (source, _) in detours.items()}
    relays = {slot: at(*middle) for slot, (_, middle) in detours.items()}

    def base(slot, part):
        return (slot * 2 + part) * heads * BLK

    def lend(slot):
        return pltpu.make_async_remote_copy(
            src_ref=send_ref.at[pl.ds(base(slot, 1), BLK)],
            dst_ref=pass_ref.at[slot],
            send_sem=send_sem.at[slot],
            recv_sem=pass_sem,
            device_id=dict(zip(("clip", "tm", "band"), detours[slot][1])),
            device_id_type=MESH,
        )

    def relay(slot):
        return pltpu.make_async_remote_copy(
            src_ref=pass_ref.at[slot],
            dst_ref=recv_ref.at[slot, 1, pl.ds(0, BLK)],
            send_sem=send_sem.at[slot],
            recv_sem=value_sem.at[0],
            device_id={"clip": 0, "tm": 0, "band": 0},
            device_id_type=MESH,
        )

    barrier = pltpu.get_barrier_semaphore()
    for axis, index, _, has_upper in neighbours:
        @pl.when(has_upper)
        def _():
            pl.semaphore_signal(barrier, inc=1, device_id={axis: index + 1}, device_id_type=MESH)

    loads = [
        pltpu.make_async_copy(source, target, load_sem.at[min(number, 3)])
        for number, (source, target) in enumerate(
            (
                (k_hbm, k_ref), (adj_hbm, adj_ref), (border_hbm, border_ref),
                (v_hbm, vq_ref.at[pl.ds(0, rows // BLK)]), (q_hbm, vq_ref.at[pl.ds(rows // BLK, rows // BLK)]),
            )
        )
    ]
    for load in loads[:3]:
        load.start()

    chunks = [[(0, heads * BLK)], value_chunks(heads)]
    skipped = BLK - FLAG

    def transfer(slot, part, group, skip=0):
        start, size = chunks[part][group]
        at = pl.ds(start + skip, size - skip)
        return pltpu.make_async_remote_copy(
            src_ref=send_ref.at[pl.ds(base(slot, part) + start + skip, size - skip)],
            dst_ref=last_recv_ref.at[slot] if group else recv_ref.at[slot, part, at],
            send_sem=send_sem.at[slot],
            recv_sem=value_sem.at[group] if part else key_sem.at[slot],
            device_id=plan[slot][0],
            device_id_type=MESH,
        )

    def ahead(slot):
        return pltpu.make_async_remote_copy(
            src_ref=k_hbm.at[:, :, pl.ds(0, HD)],
            dst_ref=both_ref.at[slot],
            send_sem=send_sem.at[slot],
            recv_sem=ahead_sem,
            device_id=plan[slot][0],
            device_id_type=MESH,
        )

    def wait(sem, size):
        some = send_ref.at[pl.ds(0, size)]
        pltpu.make_async_copy(some, some, sem).wait()

    def wait_for(conditions, sem, size):
        count = sum(jnp.int32(1) if condition is None else condition.astype(jnp.int32) for condition in conditions)
        for number in range(1, len(conditions) + 1):
            @pl.when(count == number)
            def _():
                wait(sem, number * size)

    def send(slot, part, downward):
        _, up, down, _, _, above = plan[slot]
        sends = down if downward else up
        if sends is None:
            return
        for group in range(len(chunks[part])):
            short, skip = late, skipped
            if part:
                short, skip = lends.get(slot), BLK
            if downward and group == 0 and above is not None and short is not None:
                @pl.when(sends & short)
                def _():
                    transfer(slot, part, group, skip).start()

                @pl.when(sends & jnp.logical_not(short))
                def _():
                    transfer(slot, part, group).start()
            else:
                @pl.when(sends)
                def _():
                    transfer(slot, part, group).start()

    arrivals = sum(lower.astype(jnp.int32) for _, _, lower, _ in neighbours)

    @pl.when(arrivals > 0)
    def _():
        pl.semaphore_wait(barrier, arrivals)

    for slot, (_, _, down, _, _, above) in enumerate(plan):
        if above is not None:
            @pl.when(down & late)
            def _():
                ahead(slot).start()

    for axis, index, has_lower, _ in neighbours:
        @pl.when(has_lower)
        def _():
            pl.semaphore_signal(here_sem, inc=1, device_id={axis: index - 1}, device_id_type=MESH)

    for load in loads[3:]:
        load.start()
    for load in loads[:3]:
        load.wait()
    blocks = [
        adj_ref[row, 1] if kind == "adj" else border_ref[0, row] for _, _, _, _, (kind, row), _ in plan
    ]

    def pick(slot, part, whole, start=0):
        for head in range(start, heads):
            to = base(slot, part) + head * BLK
            send_ref[to : to + BLK] = whole[blocks[slot], :, head * HD : (head + 1) * HD]

    def pick_keys(slot):
        _, _, down, _, _, above = plan[slot]
        if above is None:
            pick(slot, 0, k_ref)
            return
        pick(slot, 0, k_ref, 1)
        to = base(slot, 0)

        @pl.when(down & late)
        def _():
            send_ref[to + skipped : to + BLK] = jnp.full((FLAG, HD), blocks[slot].astype(jnp.float32)).astype(jnp.bfloat16)

        @pl.when(jnp.logical_not(down & late))
        def _():
            send_ref[to : to + BLK] = k_ref[blocks[slot], :, :HD]

    for slot in slots:
        pick_keys(slot)
        send(slot, 0, True)
    uppers = sum(upper.astype(jnp.int32) for *_, upper in neighbours)

    @pl.when(uppers > 0)
    def _():
        pl.semaphore_wait(here_sem, uppers)

    for slot in slots:
        send(slot, 0, False)

    pltpu.make_async_copy(vq_ref, vq_ref, load_sem.at[3]).wait()
    for slot in slots:
        pick(slot, 1, vq_ref)
    for slot in detours:
        @pl.when(lends[slot])
        def _():
            lend(slot).start()

    def send_values():
        for slot in slots:
            send(slot, 1, True)
            send(slot, 1, False)

    pl.when(early)(send_values)

    for slot, (_, _, _, comes, _, _) in enumerate(plan):
        if comes is not None:
            @pl.when(jnp.logical_not(comes))
            def _():
                recv_ref[slot] = jnp.zeros(recv_ref.shape[1:], recv_ref.dtype)
                last_recv_ref[slot] = jnp.zeros(last_recv_ref.shape[1:], recv_ref.dtype)

    first_last = heads - last_acc_ref.shape[0]

    def kept(head):
        if head < first_last:
            return acc_ref.at[head], weights_ref.at[head], share_ref.at[head]
        number = head - first_last
        return last_acc_ref.at[number], last_weights_ref.at[number], last_share_ref.at[number]

    def query(columns):
        return vq_ref[rows // BLK :, :, columns].reshape(rows, HD)

    own = []
    for head in range(heads):
        columns = slice(head * HD, (head + 1) * HD)
        scores = weigh(query(columns), k_ref[:, :, columns].reshape(rows, HD))
        most = jnp.max(scores, axis=1, keepdims=True)
        weights = jnp.exp2(scores - most)
        total = jnp.sum(weights, axis=1, keepdims=True)
        kept(head)[0][...] = jnp.dot(
            weights.astype(jnp.bfloat16), vq_ref[: rows // BLK, :, columns].reshape(rows, HD), preferred_element_type=jnp.float32
        )
        own.append((most, total))

    wait_for([above & late for *_, above in plan if above is not None], ahead_sem, rows)
    for slot, (_, _, _, comes, _, above) in enumerate(plan):
        if above is None:
            @when(comes)
            def _():
                transfer(slot, 0, 0).wait_recv()
        else:
            @pl.when(above & late)
            def _():
                transfer(slot, 0, 0, skipped).wait_recv()
                flag = recv_ref[slot, 0, skipped:BLK].astype(jnp.float32)
                recv_ref[slot, 0, :BLK] = jnp.where(
                    jnp.concatenate([flag] * (BLK // FLAG), axis=0) > 0.5,
                    both_ref[slot, 1].astype(jnp.float32),
                    both_ref[slot, 0].astype(jnp.float32),
                ).astype(jnp.bfloat16)

            whole = jnp.logical_not(above & late)

            @pl.when(whole if comes is None else whole & comes)
            def _():
                transfer(slot, 0, 0).wait_recv()

    for slot in detours:
        @pl.when(relays[slot])
        def _():
            lend(slot).wait_recv()
            relay(slot).start()

    pl.when(late)(send_values)

    def arrived(part, head):
        return jnp.concatenate(
            [recv_ref[slot, part, head * BLK : (head + 1) * BLK] for slot in slots], axis=0
        )

    hidden = [
        None if comes is None else jnp.where(comes, 0.0, masked_score).astype(jnp.float32)
        for _, _, _, comes, _, _ in plan
    ]
    for head in range(heads):
        columns = slice(head * HD, (head + 1) * HD)
        scores = weigh(query(columns), arrived(0, head))
        scores = [
            scores[:, slot * BLK : (slot + 1) * BLK] + (0.0 if hidden[slot] is None else hidden[slot]) for slot in slots
        ]
        most, total = own[head]
        largest = jnp.maximum(
            most, jnp.max(functools.reduce(jnp.maximum, scores), axis=1, keepdims=True)
        )
        weights = [jnp.exp2(score - largest) for score in scores]
        factor = jnp.exp2(most - largest)
        share = 1.0 / (factor * total + jnp.sum(sum(weights), axis=1, keepdims=True))
        sum_ref, part_ref, scale_ref = kept(head)
        sum_ref[...] = sum_ref[...] * factor
        scale_ref[...] = jnp.broadcast_to(share, (rows, HD))
        for slot in slots:
            part_ref[:, slot * BLK : (slot + 1) * BLK] = weights[slot].astype(jnp.bfloat16)

    for group, (start, size) in enumerate(chunks[1]):
        wait_for([comes for _, _, _, comes, _, _ in plan], value_sem.at[group], size)
        for head in range(start // BLK, min((start + size) // BLK, first_last)):
            result = acc_ref[head] + jnp.dot(
                weights_ref[head], arrived(1, head), preferred_element_type=jnp.float32
            )
            out_ref[:, head * HD : (head + 1) * HD] = (result * share_ref[head]).astype(out_ref.dtype)

    for slot, (_, up, down, _, _, above) in enumerate(plan):
        sends = down if up is None else up if down is None else None
        whole = 2 * heads * BLK
        if above is None:
            @when(sends)
            def _():
                wait(send_sem.at[slot], whole)
            continue

        longer = down & late
        passes = relays.get(slot, jnp.bool_(False))

        @pl.when(longer & passes)
        def _():
            wait(send_sem.at[slot], whole - skipped + rows + BLK)

        @pl.when(longer & jnp.logical_not(passes))
        def _():
            wait(send_sem.at[slot], whole - skipped + rows)

        plain = jnp.logical_not(longer)

        @pl.when(plain if sends is None else plain & sends)
        def _():
            wait(send_sem.at[slot], whole)


def finish(done_ref, acc_ref, weights_ref, share_ref, recv_ref, out_hbm, last_ref, sem):
    width = done_ref.shape[1]
    copies = [
        pltpu.make_async_copy(done_ref, out_hbm.at[:, pl.ds(0, width)], sem.at[0]),
        pltpu.make_async_copy(last_ref, out_hbm.at[:, pl.ds(width, last_ref.shape[1])], sem.at[1]),
    ]
    copies[0].start()
    for head in range(acc_ref.shape[0]):
        values = jnp.concatenate(
            [recv_ref[slot, head * BLK : (head + 1) * BLK] for slot in range(recv_ref.shape[0])], axis=0
        )
        result = acc_ref[head] + jnp.dot(weights_ref[head], values, preferred_element_type=jnp.float32)
        last_ref[:, head * HD : (head + 1) * HD] = (result * share_ref[head]).astype(last_ref.dtype)
    copies[1].start()
    for copy in copies:
        copy.wait()


def per_device(queries, keys, values, adj_mask, border_blocks):
    rows, width = queries.shape[2:]
    heads = width // HD
    clip_count, slab_count, band_count = (lax.axis_size(axis) for axis in ("clip", "tm", "band"))
    sources = (2 if slab_count > 1 else 0) + min(band_count - 1, 2)
    assert rows == 2 * BLK and adj_mask.shape[3] == 2 and border_blocks.shape[3] == 1
    last = last_heads(heads)
    parts = pl.pallas_call(
        functools.partial(kernel, clip_count, slab_count, band_count),
        out_shape=[
            pltpu.VMEM((rows, width - last * HD), jnp.bfloat16),
            pltpu.VMEM((last, rows, HD), jnp.float32),
            pltpu.VMEM((last, rows, sources * BLK), jnp.bfloat16),
            pltpu.VMEM((last, rows, HD), jnp.float32),
            pltpu.VMEM((sources, last * BLK, HD), jnp.bfloat16),
        ],
        in_specs=[pl.BlockSpec(memory_space=pl.ANY)] * 5,
        out_specs=[pl.BlockSpec(memory_space=pltpu.VMEM)] * 5,
        scratch_shapes=[
            pltpu.VMEM((2 * rows // BLK, BLK, width), jnp.bfloat16),
            pltpu.VMEM((rows // BLK, BLK, width), jnp.bfloat16),
            pltpu.SMEM(adj_mask.shape[2:], jnp.int32),
            pltpu.SMEM(border_blocks.shape[:1:-1], jnp.int32),
            pltpu.VMEM(((sources + 1) * 2 * heads * BLK, HD), jnp.bfloat16),
            pltpu.VMEM((sources, 2, heads * BLK, HD), jnp.bfloat16),
            pltpu.VMEM((heads, rows, HD), jnp.float32),
            pltpu.VMEM((heads, rows, sources * BLK), jnp.bfloat16),
            pltpu.VMEM((heads, rows, HD), jnp.float32),
            pltpu.VMEM((sources, rows // BLK, BLK, HD), jnp.bfloat16),
            pltpu.VMEM((sources, BLK, HD), jnp.bfloat16),
            pltpu.SemaphoreType.DMA((4,)),
            pltpu.SemaphoreType.REGULAR,
            pltpu.SemaphoreType.DMA((sources,)),
            pltpu.SemaphoreType.DMA,
            pltpu.SemaphoreType.DMA,
            pltpu.SemaphoreType.DMA((sources,)),
            pltpu.SemaphoreType.DMA((2,)),
        ],
        compiler_params=pltpu.CompilerParams(collective_id=0, has_side_effects=True),
        name="radial_attention",
    )(
        queries.reshape(rows // BLK, BLK, width),
        keys.reshape(rows // BLK, BLK, width),
        values.reshape(rows // BLK, BLK, width),
        adj_mask[0, 0], border_blocks[0, 0].T,
    )
    attended = pl.pallas_call(
        finish,
        out_shape=jax.ShapeDtypeStruct((rows, width), jnp.bfloat16),
        in_specs=[pl.BlockSpec(memory_space=pltpu.VMEM)] * 5,
        out_specs=pl.BlockSpec(memory_space=pl.ANY),
        scratch_shapes=[pltpu.VMEM((rows, last * HD), jnp.bfloat16), pltpu.SemaphoreType.DMA((2,))],
        name="last_heads",
    )(*(pltpu.with_memory_space_constraint(part, pltpu.VMEM) for part in parts))
    return attended[None, None]


def solution(mesh):
    placed = (
        P(("clip", "tm"), "band", None, "head"),
        P(("clip", "tm"), "band", None, "head"),
        P(("clip", "tm"), "band", None, "head"),
        P(("clip", "tm"), "band", None, None),
        P(("clip", "tm"), "band", None, None),
    )
    return jax.shard_map(
        per_device,
        mesh=mesh,
        in_specs=placed,
        out_specs=P(("clip", "tm"), "band", None, "head"),
        check_vma=False,
    )
```

```python
import functools
import math

import jax
import jax.numpy as jnp
from jax import lax
from jax.experimental import pallas as pl
from jax.experimental.pallas import tpu as pltpu
from jax.sharding import PartitionSpec as P

BLK = 128
HD = 128

masked_score = -1e30
SCALE2 = math.log2(math.e) / math.sqrt(HD)
MESH = pl.DeviceIdType.MESH
TAIL = 1

ROUTE_X = ((0, 0, 1), (1, 0, 1))
ROUTE_Z = ((0, 1, 0), (1, 1, 0))


def routes(slab_count, band_count):
    slab, band = lax.axis_index("tm"), lax.axis_index("band")
    found = []
    if slab_count > 1:
        found.append(({"tm": slab - 1}, None, slab > 0, slab < slab_count - 1, ("adj", 1), slab < slab_count - 1))
    if band_count == 2:
        found.append(({"band": 1 - band}, band == 0, band == 1, None, ("border", 1 - band), band == 0))
    elif band_count > 2:
        found.append(({"band": band - 1}, None, band > 0, band < band_count - 1, ("border", 0), band < band_count - 1))
        found.append(({"band": band + 1}, band < band_count - 1, None, band > 0, ("border", 1), None))
    if slab_count > 1:
        found.append(({"tm": slab + 1}, slab < slab_count - 1, None, slab > 0, ("adj", 0), None))
    return found


def when(condition):
    return (lambda body: body()) if condition is None else pl.when(condition)


def last_heads(heads):
    return TAIL if heads > 2 * TAIL else 1


def value_chunks(heads):
    most = heads - last_heads(heads)
    return [(0, most * BLK), (most * BLK, (heads - most) * BLK)]


FLAG = 16


def weigh(query, key):
    scores = lax.dot_general(
        query, key, (((1,), (1,)), ((), ())), preferred_element_type=jnp.float32
    )
    return scores * SCALE2


def kernel(
    clip_count, slab_count, band_count, q_hbm, k_hbm, v_hbm, adj_hbm, border_hbm,
    out_ref, last_acc_ref, last_weights_ref, last_share_ref, values_ref,
    vq_ref, k_ref, adj_ref, border_ref, send_ref, recv_ref, acc_ref, weights_ref, share_ref,
    both_ref, pass_ref,
    load_sem, here_sem, send_sem, ahead_sem, pass_sem, key_sem, value_sem,
):
    plan = routes(slab_count, band_count)
    slots = range(len(plan))
    rows, width = k_ref.shape[0] * BLK, k_ref.shape[2]
    heads = width // HD
    late = lax.axis_index("head") > 0
    early = jnp.logical_not(late)

    neighbours = []
    for axis, count in (("tm", slab_count), ("band", band_count), ("clip", clip_count)):
        if count > 1:
            index = lax.axis_index(axis)
            lower, upper = index > 0, index < count - 1
            if axis == "clip":
                lower, upper = lower & late, upper & late
            neighbours.append((axis, index, lower, upper))

    detours = {}
    if clip_count > 1 and slab_count > 1 and band_count > 1:
        for slot, (_, _, _, _, (kind, _), above) in enumerate(plan):
            if above is not None:
                detours[slot] = ROUTE_X if kind == "border" else ROUTE_Z

    def at(clip, slab, band):
        place = [lax.axis_index(axis) for axis in ("clip", "tm", "band")]
        return (place[0] == clip) & (place[1] == slab) & (place[2] == band) & late

    lends = {slot: at(*source) for slot, (source, _) in detours.items()}
    relays = {slot: at(*middle) for slot, (_, middle) in detours.items()}

    owns = [slot for slot, (*_, above) in enumerate(plan) if above is not None]
    takes = [slot for slot, (*_, above) in enumerate(plan) if above is None]

    def sent(slot):
        return send_sem.at[owns.index(slot)] if slot in owns else load_sem.at[takes.index(slot)]

    def base(slot, part):
        return (slot * 2 + part) * heads * BLK

    def lend(slot):
        return pltpu.make_async_remote_copy(
            src_ref=send_ref.at[pl.ds(base(slot, 1), BLK)],
            dst_ref=pass_ref.at[slot],
            send_sem=sent(slot),
            recv_sem=pass_sem,
            device_id=dict(zip(("clip", "tm", "band"), detours[slot][1])),
            device_id_type=MESH,
        )

    def relay(slot):
        return pltpu.make_async_remote_copy(
            src_ref=pass_ref.at[slot],
            dst_ref=values_ref.at[slot, pl.ds(0, BLK)],
            send_sem=sent(slot),
            recv_sem=value_sem.at[0],
            device_id={"clip": 0, "tm": 0, "band": 0},
            device_id_type=MESH,
        )

    barrier = pltpu.get_barrier_semaphore()
    for axis, index, _, has_upper in neighbours:
        @pl.when(has_upper)
        def _():
            pl.semaphore_signal(barrier, inc=1, device_id={axis: index + 1}, device_id_type=MESH)

    loads = [
        pltpu.make_async_copy(source, target, load_sem.at[min(number, 3)])
        for number, (source, target) in enumerate(
            (
                (k_hbm, k_ref), (adj_hbm, adj_ref), (border_hbm, border_ref),
                (v_hbm, vq_ref.at[pl.ds(0, rows // BLK)]), (q_hbm, vq_ref.at[pl.ds(rows // BLK, rows // BLK)]),
            )
        )
    ]
    for load in loads[:3]:
        load.start()

    chunks = [[(0, heads * BLK)], value_chunks(heads)]
    skipped = BLK - FLAG

    def transfer(slot, part, group, skip=0, whole=False):
        start, size = (0, heads * BLK) if whole else chunks[part][group]
        at = pl.ds(start + skip, size - skip)
        return pltpu.make_async_remote_copy(
            src_ref=send_ref.at[pl.ds(base(slot, part) + start + skip, size - skip)],
            dst_ref=values_ref.at[slot, at] if part else recv_ref.at[slot, at],
            send_sem=sent(slot),
            recv_sem=value_sem.at[group] if part else key_sem.at[slot],
            device_id=plan[slot][0],
            device_id_type=MESH,
        )

    def ahead(slot):
        return pltpu.make_async_remote_copy(
            src_ref=k_hbm.at[:, :, pl.ds(0, HD)],
            dst_ref=both_ref.at[slot],
            send_sem=sent(slot),
            recv_sem=ahead_sem,
            device_id=plan[slot][0],
            device_id_type=MESH,
        )

    def wait(sem, size):
        some = send_ref.at[pl.ds(0, size)]
        pltpu.make_async_copy(some, some, sem).wait()

    def wait_for(conditions, sem, size):
        count = sum(jnp.int32(1) if condition is None else condition.astype(jnp.int32) for condition in conditions)
        for number in range(1, len(conditions) + 1):
            @pl.when(count == number)
            def _():
                wait(sem, number * size)

    def send(slot, part, downward):
        _, up, down, _, _, above = plan[slot]
        sends = down if downward else up
        if sends is None:
            return
        for group in range(len(chunks[part])):
            short, skip = late, skipped
            if part:
                short, skip = lends.get(slot), BLK
            if downward and group == 0 and above is not None and short is not None:
                @pl.when(sends & short)
                def _():
                    transfer(slot, part, group, skip).start()

                @pl.when(sends & jnp.logical_not(short))
                def _():
                    transfer(slot, part, group).start()
            else:
                @pl.when(sends)
                def _():
                    transfer(slot, part, group).start()

    arrivals = sum(lower.astype(jnp.int32) for _, _, lower, _ in neighbours)

    @pl.when(arrivals > 0)
    def _():
        pl.semaphore_wait(barrier, arrivals)

    for slot, (_, _, down, _, _, above) in enumerate(plan):
        if above is not None:
            @pl.when(down & late)
            def _():
                ahead(slot).start()

    for axis, index, has_lower, _ in neighbours:
        @pl.when(has_lower)
        def _():
            pl.semaphore_signal(here_sem, inc=1, device_id={axis: index - 1}, device_id_type=MESH)

    for load in loads[3:]:
        load.start()
    for load in loads[:3]:
        load.wait()
    blocks = [
        adj_ref[row, 1] if kind == "adj" else border_ref[0, row] for _, _, _, _, (kind, row), _ in plan
    ]

    def pick(slot, part, whole, start=0):
        for head in range(start, heads):
            to = base(slot, part) + head * BLK
            send_ref[to : to + BLK] = whole[blocks[slot], :, head * HD : (head + 1) * HD]

    def pick_keys(slot):
        _, _, down, _, _, above = plan[slot]
        if above is None:
            pick(slot, 0, k_ref)
            return
        pick(slot, 0, k_ref, 1)
        to = base(slot, 0)

        @pl.when(down & late)
        def _():
            send_ref[to + skipped : to + BLK] = jnp.full((FLAG, HD), blocks[slot].astype(jnp.float32)).astype(jnp.bfloat16)

        @pl.when(jnp.logical_not(down & late))
        def _():
            send_ref[to : to + BLK] = k_ref[blocks[slot], :, :HD]

    for slot in slots:
        pick_keys(slot)
        send(slot, 0, True)
    uppers = sum(upper.astype(jnp.int32) for *_, upper in neighbours)

    @pl.when(uppers > 0)
    def _():
        pl.semaphore_wait(here_sem, uppers)

    for slot in slots:
        send(slot, 0, False)

    pltpu.make_async_copy(vq_ref, vq_ref, load_sem.at[3]).wait()
    for slot in slots:
        pick(slot, 1, vq_ref)
    for slot in detours:
        @pl.when(lends[slot])
        def _():
            lend(slot).start()

    def send_values():
        for slot in slots:
            send(slot, 1, True)
            send(slot, 1, False)

    for slot, (_, up, down, _, _, _) in enumerate(plan):
        @pl.when(early & (down if up is None else up if down is None else up | down))
        def _():
            transfer(slot, 1, 0, whole=True).start()

    for slot, (_, _, _, comes, _, _) in enumerate(plan):
        if comes is not None:
            @pl.when(jnp.logical_not(comes))
            def _():
                recv_ref[slot] = jnp.zeros(recv_ref.shape[1:], recv_ref.dtype)
                values_ref[slot] = jnp.zeros(values_ref.shape[1:], values_ref.dtype)

    first_last = heads - last_acc_ref.shape[0]

    def kept(head):
        if head < first_last:
            return acc_ref.at[head], weights_ref.at[head], share_ref.at[head]
        number = head - first_last
        return last_acc_ref.at[number], last_weights_ref.at[number], last_share_ref.at[number]

    def query(columns):
        return vq_ref[rows // BLK :, :, columns].reshape(rows, HD)

    own = []
    for head in range(heads):
        columns = slice(head * HD, (head + 1) * HD)
        scores = weigh(query(columns), k_ref[:, :, columns].reshape(rows, HD))
        most = jnp.max(scores, axis=1, keepdims=True)
        weights = jnp.exp2(scores - most)
        total = jnp.sum(weights, axis=1, keepdims=True)
        kept(head)[0][...] = jnp.dot(
            weights.astype(jnp.bfloat16), vq_ref[: rows // BLK, :, columns].reshape(rows, HD), preferred_element_type=jnp.float32
        )
        own.append((most, total))

    wait_for([above & late for *_, above in plan if above is not None], ahead_sem, rows)
    for slot, (_, _, _, comes, _, above) in enumerate(plan):
        if above is None:
            @when(comes)
            def _():
                transfer(slot, 0, 0).wait_recv()
        else:
            @pl.when(above & late)
            def _():
                transfer(slot, 0, 0, skipped).wait_recv()
                flag = recv_ref[slot, skipped:BLK].astype(jnp.float32)
                recv_ref[slot, :BLK] = jnp.where(
                    jnp.concatenate([flag] * (BLK // FLAG), axis=0) > 0.5,
                    both_ref[slot, 1].astype(jnp.float32),
                    both_ref[slot, 0].astype(jnp.float32),
                ).astype(jnp.bfloat16)

            whole = jnp.logical_not(above & late)

            @pl.when(whole if comes is None else whole & comes)
            def _():
                transfer(slot, 0, 0).wait_recv()

    for slot in detours:
        @pl.when(relays[slot])
        def _():
            lend(slot).wait_recv()
            relay(slot).start()

    pl.when(late)(send_values)

    def arrived(ref, head):
        return jnp.concatenate([ref[slot, head * BLK : (head + 1) * BLK] for slot in slots], axis=0)

    hidden = [
        None if comes is None else jnp.where(comes, 0.0, masked_score).astype(jnp.float32)
        for _, _, _, comes, _, _ in plan
    ]
    for head in range(heads):
        columns = slice(head * HD, (head + 1) * HD)
        scores = weigh(query(columns), arrived(recv_ref, head))
        scores = [
            scores[:, slot * BLK : (slot + 1) * BLK] + (0.0 if hidden[slot] is None else hidden[slot]) for slot in slots
        ]
        most, total = own[head]
        largest = jnp.maximum(
            most, jnp.max(functools.reduce(jnp.maximum, scores), axis=1, keepdims=True)
        )
        weights = [jnp.exp2(score - largest) for score in scores]
        factor = jnp.exp2(most - largest)
        share = 1.0 / (factor * total + jnp.sum(sum(weights), axis=1, keepdims=True))
        sum_ref, part_ref, scale_ref = kept(head)
        sum_ref[...] = sum_ref[...] * factor
        scale_ref[...] = jnp.broadcast_to(share, (rows, HD))
        for slot in slots:
            part_ref[:, slot * BLK : (slot + 1) * BLK] = weights[slot].astype(jnp.bfloat16)

    def came(role):
        return [role if comes is None else role & comes for _, _, _, comes, _, _ in plan]

    for group, (start, size) in enumerate(chunks[1]):
        if group == 0:
            wait_for(came(early), value_sem.at[group], heads * BLK)
        wait_for(came(late), value_sem.at[group], size)
        for head in range(start // BLK, min((start + size) // BLK, first_last)):
            result = acc_ref[head] + jnp.dot(
                weights_ref[head], arrived(values_ref, head), preferred_element_type=jnp.float32
            )
            out_ref[:, head * HD : (head + 1) * HD] = (result * share_ref[head]).astype(out_ref.dtype)

    for slot, (_, up, down, _, _, above) in enumerate(plan):
        sends = down if up is None else up if down is None else None
        whole = 2 * heads * BLK
        if above is None:
            @when(sends)
            def _():
                wait(sent(slot), whole)
            continue

        longer = down & late
        passes = relays.get(slot, jnp.bool_(False))

        @pl.when(longer & passes)
        def _():
            wait(sent(slot), whole - skipped + rows + BLK)

        @pl.when(longer & jnp.logical_not(passes))
        def _():
            wait(sent(slot), whole - skipped + rows)

        plain = jnp.logical_not(longer)

        @pl.when(plain if sends is None else plain & sends)
        def _():
            wait(sent(slot), whole)


def finish(done_ref, acc_ref, weights_ref, share_ref, values_ref, out_hbm, last_ref, sem):
    width = done_ref.shape[1]
    first = width // HD
    pltpu.make_async_copy(done_ref, out_hbm.at[:, pl.ds(0, width)], sem).start()
    for head in range(acc_ref.shape[0]):
        values = jnp.concatenate(
            [
                values_ref[slot, (first + head) * BLK : (first + head + 1) * BLK]
                for slot in range(values_ref.shape[0])
            ],
            axis=0,
        )
        result = acc_ref[head] + jnp.dot(weights_ref[head], values, preferred_element_type=jnp.float32)
        last_ref[:, head * HD : (head + 1) * HD] = (result * share_ref[head]).astype(last_ref.dtype)
    pltpu.make_async_copy(last_ref, out_hbm.at[:, pl.ds(width, last_ref.shape[1])], sem).start()
    pltpu.make_async_copy(out_hbm, out_hbm, sem).wait()


def per_device(queries, keys, values, adj_mask, border_blocks):
    rows, width = queries.shape[2:]
    heads = width // HD
    clip_count, slab_count, band_count = (lax.axis_size(axis) for axis in ("clip", "tm", "band"))
    sources = (2 if slab_count > 1 else 0) + min(band_count - 1, 2)
    assert rows == 2 * BLK and adj_mask.shape[3] == 2 and border_blocks.shape[3] == 1
    last = last_heads(heads)
    parts = pl.pallas_call(
        functools.partial(kernel, clip_count, slab_count, band_count),
        out_shape=[
            pltpu.VMEM((rows, width - last * HD), jnp.bfloat16),
            pltpu.VMEM((last, rows, HD), jnp.float32),
            pltpu.VMEM((last, rows, sources * BLK), jnp.bfloat16),
            pltpu.VMEM((last, rows, HD), jnp.float32),
            pltpu.VMEM((sources, heads * BLK, HD), jnp.bfloat16),
        ],
        in_specs=[pl.BlockSpec(memory_space=pl.ANY)] * 5,
        out_specs=[pl.BlockSpec(memory_space=pltpu.VMEM)] * 5,
        scratch_shapes=[
            pltpu.VMEM((2 * rows // BLK, BLK, width), jnp.bfloat16),
            pltpu.VMEM((rows // BLK, BLK, width), jnp.bfloat16),
            pltpu.SMEM(adj_mask.shape[2:], jnp.int32),
            pltpu.SMEM(border_blocks.shape[:1:-1], jnp.int32),
            pltpu.VMEM(((sources + 1) * 2 * heads * BLK, HD), jnp.bfloat16),
            pltpu.VMEM((sources, heads * BLK, HD), jnp.bfloat16),
            pltpu.VMEM((heads, rows, HD), jnp.float32),
            pltpu.VMEM((heads, rows, sources * BLK), jnp.bfloat16),
            pltpu.VMEM((heads, rows, HD), jnp.float32),
            pltpu.VMEM((sources, rows // BLK, BLK, HD), jnp.bfloat16),
            pltpu.VMEM((sources, BLK, HD), jnp.bfloat16),
            pltpu.SemaphoreType.DMA((4,)),
            pltpu.SemaphoreType.REGULAR,
            pltpu.SemaphoreType.DMA(((slab_count > 1) + (band_count > 1),)),
            pltpu.SemaphoreType.DMA,
            pltpu.SemaphoreType.DMA,
            pltpu.SemaphoreType.DMA((sources,)),
            pltpu.SemaphoreType.DMA((2,)),
        ],
        compiler_params=pltpu.CompilerParams(collective_id=0, has_side_effects=True),
        name="radial_attention",
    )(
        queries.reshape(rows // BLK, BLK, width),
        keys.reshape(rows // BLK, BLK, width),
        values.reshape(rows // BLK, BLK, width),
        adj_mask[0, 0], border_blocks[0, 0].T,
    )
    attended = pl.pallas_call(
        finish,
        out_shape=jax.ShapeDtypeStruct((rows, width), jnp.bfloat16),
        in_specs=[pl.BlockSpec(memory_space=pltpu.VMEM)] * 5,
        out_specs=pl.BlockSpec(memory_space=pl.ANY),
        scratch_shapes=[pltpu.VMEM((rows, last * HD), jnp.bfloat16), pltpu.SemaphoreType.DMA],
        name="last_heads",
    )(*(pltpu.with_memory_space_constraint(part, pltpu.VMEM) for part in parts))
    return attended[None, None]


def solution(mesh):
    placed = (
        P(("clip", "tm"), "band", None, "head"),
        P(("clip", "tm"), "band", None, "head"),
        P(("clip", "tm"), "band", None, "head"),
        P(("clip", "tm"), "band", None, None),
        P(("clip", "tm"), "band", None, None),
    )
    return jax.shard_map(
        per_device,
        mesh=mesh,
        in_specs=placed,
        out_specs=P(("clip", "tm"), "band", None, "head"),
        check_vma=False,
    )
```

```python
import functools
import math

import jax
import jax.numpy as jnp
from jax import lax
from jax.experimental import pallas as pl
from jax.experimental.pallas import tpu as pltpu
from jax.sharding import PartitionSpec as P

BLK = 128
HD = 128

masked_score = -1e30
SCALE2 = math.log2(math.e) / math.sqrt(HD)
MESH = pl.DeviceIdType.MESH
TAIL = 1

ROUTE_X = ((0, 0, 1), (1, 0, 1))
ROUTE_Z = ((0, 1, 0), (1, 1, 0))


def routes(slab_count, band_count):
    slab, band = lax.axis_index("tm"), lax.axis_index("band")
    found = []
    if slab_count > 1:
        found.append(({"tm": slab - 1}, None, slab > 0, slab < slab_count - 1, ("adj", 1), slab < slab_count - 1))
    if band_count == 2:
        found.append(({"band": 1 - band}, band == 0, band == 1, None, ("border", 1 - band), band == 0))
    elif band_count > 2:
        found.append(({"band": band - 1}, None, band > 0, band < band_count - 1, ("border", 0), band < band_count - 1))
        found.append(({"band": band + 1}, band < band_count - 1, None, band > 0, ("border", 1), None))
    if slab_count > 1:
        found.append(({"tm": slab + 1}, slab < slab_count - 1, None, slab > 0, ("adj", 0), None))
    return found


def when(condition):
    return (lambda body: body()) if condition is None else pl.when(condition)


def last_heads(heads):
    return TAIL if heads > 2 * TAIL else 1


def value_chunks(heads):
    most = heads - last_heads(heads)
    return [(0, most * BLK), (most * BLK, (heads - most) * BLK)]


FLAG = 8


def weigh(query, key):
    scores = lax.dot_general(
        query, key, (((1,), (1,)), ((), ())), preferred_element_type=jnp.float32
    )
    return scores * SCALE2


def kernel(
    clip_count, slab_count, band_count, q_hbm, k_hbm, v_hbm, adj_hbm, border_hbm,
    out_ref, last_acc_ref, last_weights_ref, last_share_ref, values_ref,
    vq_ref, k_ref, adj_ref, border_ref, send_ref, recv_ref, acc_ref, weights_ref, share_ref,
    both_ref, pass_ref,
    load_sem, here_sem, ahead_sem, pass_sem, key_sem, value_sem,
):
    rows, width = k_ref.shape[0] * BLK, k_ref.shape[2]
    loads = [
        pltpu.make_async_copy(source, target, load_sem.at[min(number, 3)])
        for number, (source, target) in enumerate(
            (
                (k_hbm, k_ref), (adj_hbm, adj_ref), (border_hbm, border_ref),
                (v_hbm, vq_ref.at[pl.ds(0, rows // BLK)]), (q_hbm, vq_ref.at[pl.ds(rows // BLK, rows // BLK)]),
            )
        )
    ]
    for load in loads[:3]:
        load.start()

    plan = routes(slab_count, band_count)
    slots = range(len(plan))
    heads = width // HD
    late = lax.axis_index("head") > 0
    early = jnp.logical_not(late)

    neighbours = []
    for axis, count in (("tm", slab_count), ("band", band_count), ("clip", clip_count)):
        if count > 1:
            index = lax.axis_index(axis)
            lower, upper = index > 0, index < count - 1
            if axis == "clip":
                lower, upper = lower & late, upper & late
            neighbours.append((axis, index, lower, upper))

    detours = {}
    if clip_count > 1 and slab_count > 1 and band_count > 1:
        for slot, (_, _, _, _, (kind, _), above) in enumerate(plan):
            if above is not None:
                detours[slot] = ROUTE_X if kind == "border" else ROUTE_Z

    def at(clip, slab, band):
        place = [lax.axis_index(axis) for axis in ("clip", "tm", "band")]
        return (place[0] == clip) & (place[1] == slab) & (place[2] == band) & late

    lends = {slot: at(*source) for slot, (source, _) in detours.items()}
    relays = {slot: at(*middle) for slot, (_, middle) in detours.items()}

    def sent(slot):
        return load_sem.at[slot if slot < 3 else slot + 1]

    def base(slot, part):
        return (slot * 2 + part) * heads * BLK

    def lend(slot):
        return pltpu.make_async_remote_copy(
            src_ref=send_ref.at[pl.ds(base(slot, 1), BLK)],
            dst_ref=pass_ref.at[slot],
            send_sem=sent(slot),
            recv_sem=pass_sem,
            device_id=dict(zip(("clip", "tm", "band"), detours[slot][1])),
            device_id_type=MESH,
        )

    def relay(slot):
        return pltpu.make_async_remote_copy(
            src_ref=pass_ref.at[slot],
            dst_ref=values_ref.at[slot, pl.ds(0, BLK)],
            send_sem=sent(slot),
            recv_sem=value_sem.at[0],
            device_id={"clip": 0, "tm": 0, "band": 0},
            device_id_type=MESH,
        )

    barrier = pltpu.get_barrier_semaphore()
    for axis, index, _, has_upper in neighbours:
        @pl.when(has_upper)
        def _():
            pl.semaphore_signal(barrier, inc=1, device_id={axis: index + 1}, device_id_type=MESH)

    chunks = [[(0, heads * BLK)], value_chunks(heads)]
    skipped = BLK - FLAG

    def transfer(slot, part, group, skip=0, whole=False):
        start, size = (0, heads * BLK) if whole else chunks[part][group]
        at = pl.ds(start + skip, size - skip)
        return pltpu.make_async_remote_copy(
            src_ref=send_ref.at[pl.ds(base(slot, part) + start + skip, size - skip)],
            dst_ref=values_ref.at[slot, at] if part else recv_ref.at[slot, at],
            send_sem=sent(slot),
            recv_sem=value_sem.at[group] if part else key_sem,
            device_id=plan[slot][0],
            device_id_type=MESH,
        )

    def ahead(slot):
        return pltpu.make_async_remote_copy(
            src_ref=k_hbm.at[:, :, pl.ds(0, HD)],
            dst_ref=both_ref.at[slot],
            send_sem=ahead_sem,
            recv_sem=key_sem,
            device_id=plan[slot][0],
            device_id_type=MESH,
        )

    def wait(sem, size):
        some = send_ref.at[pl.ds(0, size)]
        pltpu.make_async_copy(some, some, sem).wait()

    def wait_for(conditions, sem, size):
        count = sum(jnp.int32(1) if condition is None else condition.astype(jnp.int32) for condition in conditions)
        for number in range(1, len(conditions) + 1):
            @pl.when(count == number)
            def _():
                wait(sem, number * size)

    def send(slot, part, downward):
        _, up, down, _, _, above = plan[slot]
        sends = down if downward else up
        if sends is None:
            return
        for group in range(len(chunks[part])):
            short, skip = late, skipped
            if part:
                short, skip = lends.get(slot), BLK
            if downward and group == 0 and above is not None and short is not None:
                @pl.when(sends & short)
                def _():
                    transfer(slot, part, group, skip).start()

                @pl.when(sends & jnp.logical_not(short))
                def _():
                    transfer(slot, part, group).start()
            else:
                @pl.when(sends)
                def _():
                    transfer(slot, part, group).start()

    arrivals = sum(lower.astype(jnp.int32) for _, _, lower, _ in neighbours)

    @pl.when(arrivals > 0)
    def _():
        pl.semaphore_wait(barrier, arrivals)

    for slot, (_, _, down, _, _, above) in enumerate(plan):
        if above is not None:
            @pl.when(down & late)
            def _():
                ahead(slot).start()

    for axis, index, has_lower, _ in neighbours:
        @pl.when(has_lower)
        def _():
            pl.semaphore_signal(here_sem, inc=1, device_id={axis: index - 1}, device_id_type=MESH)

    for load in loads[3:]:
        load.start()
    for load in loads[:3]:
        load.wait()
    blocks = [
        adj_ref[row, 1] if kind == "adj" else border_ref[0, row] for _, _, _, _, (kind, row), _ in plan
    ]

    def pick(slot, part, whole, start=0):
        for head in range(start, heads):
            to = base(slot, part) + head * BLK
            send_ref[to : to + BLK] = whole[blocks[slot], :, head * HD : (head + 1) * HD]

    def sends(slot):
        _, up, down, _, _, _ = plan[slot]
        return down if up is None else up if down is None else None

    def pick_keys(slot):
        _, _, down, _, _, above = plan[slot]
        if above is None:
            when(sends(slot))(lambda: pick(slot, 0, k_ref))
            return
        when(sends(slot))(lambda: pick(slot, 0, k_ref, 1))
        to = base(slot, 0)

        @pl.when(down & late)
        def _():
            send_ref[to + skipped : to + BLK] = jnp.full((FLAG, HD), blocks[slot].astype(jnp.float32)).astype(jnp.bfloat16)

        @pl.when(jnp.logical_not(down & late))
        def _():
            send_ref[to : to + BLK] = k_ref[blocks[slot], :, :HD]

    for slot in slots:
        pick_keys(slot)
        send(slot, 0, True)
    uppers = sum(upper.astype(jnp.int32) for *_, upper in neighbours)

    @pl.when(uppers > 0)
    def _():
        pl.semaphore_wait(here_sem, uppers)

    for slot in slots:
        send(slot, 0, False)

    pltpu.make_async_copy(vq_ref, vq_ref, load_sem.at[3]).wait()
    for slot in slots:
        when(sends(slot))(functools.partial(pick, slot, 1, vq_ref))
    for slot in detours:
        @pl.when(lends[slot])
        def _():
            lend(slot).start()

    def send_values():
        for slot in slots:
            send(slot, 1, True)
            send(slot, 1, False)

    for slot, (_, up, down, _, _, _) in enumerate(plan):
        @pl.when(early & (down if up is None else up if down is None else up | down))
        def _():
            transfer(slot, 1, 0, whole=True).start()

    for slot, (_, _, _, comes, _, _) in enumerate(plan):
        if comes is not None:
            @pl.when(jnp.logical_not(comes))
            def _():
                recv_ref[slot] = jnp.zeros(recv_ref.shape[1:], recv_ref.dtype)
                values_ref[slot] = jnp.zeros(values_ref.shape[1:], values_ref.dtype)

    first_last = heads - last_acc_ref.shape[0]

    def kept(head):
        if head < first_last:
            return acc_ref.at[head], weights_ref.at[head], share_ref.at[head]
        number = head - first_last
        return last_acc_ref.at[number], last_weights_ref.at[number], last_share_ref.at[number]

    def query(columns):
        return vq_ref[rows // BLK :, :, columns].reshape(rows, HD)

    own = []
    for head in range(heads):
        columns = slice(head * HD, (head + 1) * HD)
        scores = weigh(query(columns), k_ref[:, :, columns].reshape(rows, HD))
        most = jnp.max(scores, axis=1, keepdims=True)
        weights = jnp.exp2(scores - most)
        total = jnp.sum(weights, axis=1, keepdims=True)
        kept(head)[0][...] = jnp.dot(
            weights.astype(jnp.bfloat16), vq_ref[: rows // BLK, :, columns].reshape(rows, HD), preferred_element_type=jnp.float32
        )
        own.append((most, total))

    ones = [above & late for *_, above in plan if above is not None]
    shorter = sum(one.astype(jnp.int32) for one in ones)
    longer = (
        sum(jnp.int32(1) if comes is None else comes.astype(jnp.int32) for _, _, _, comes, _, _ in plan) - shorter
    )
    for some in range(len(ones) + 1):
        for more in range(len(plan) + 1 - some):
            if some + more:
                @pl.when((shorter == some) & (longer == more))
                def _():
                    wait(key_sem, some * (heads * BLK - skipped + rows) + more * heads * BLK)

    for slot, (*_, above) in enumerate(plan):
        if above is not None:
            @pl.when(above & late)
            def _():
                flag = recv_ref[slot, skipped:BLK].astype(jnp.float32)
                recv_ref[slot, :BLK] = jnp.where(
                    jnp.concatenate([flag] * (BLK // FLAG), axis=0) > 0.5,
                    both_ref[slot, 1].astype(jnp.float32),
                    both_ref[slot, 0].astype(jnp.float32),
                ).astype(jnp.bfloat16)

    wait_for([down & late for _, _, down, _, _, above in plan if above is not None], ahead_sem, rows)

    for slot in detours:
        @pl.when(relays[slot])
        def _():
            lend(slot).wait_recv()
            relay(slot).start()

    pl.when(late)(send_values)

    def arrived(ref, head):
        return jnp.concatenate([ref[slot, head * BLK : (head + 1) * BLK] for slot in slots], axis=0)

    hidden = [
        None if comes is None else jnp.where(comes, 0.0, masked_score).astype(jnp.float32)
        for _, _, _, comes, _, _ in plan
    ]
    for head in range(heads):
        columns = slice(head * HD, (head + 1) * HD)
        scores = weigh(query(columns), arrived(recv_ref, head))
        scores = [
            scores[:, slot * BLK : (slot + 1) * BLK] + (0.0 if hidden[slot] is None else hidden[slot]) for slot in slots
        ]
        most, total = own[head]
        largest = jnp.maximum(
            most, jnp.max(functools.reduce(jnp.maximum, scores), axis=1, keepdims=True)
        )
        weights = [jnp.exp2(score - largest) for score in scores]
        factor = jnp.exp2(most - largest)
        share = 1.0 / (factor * total + jnp.sum(sum(weights), axis=1, keepdims=True))
        sum_ref, part_ref, scale_ref = kept(head)
        sum_ref[...] = sum_ref[...] * factor
        scale_ref[...] = jnp.broadcast_to(share, (rows, HD))
        for slot in slots:
            part_ref[:, slot * BLK : (slot + 1) * BLK] = weights[slot].astype(jnp.bfloat16)

    def came(role):
        return [role if comes is None else role & comes for _, _, _, comes, _, _ in plan]

    for group, (start, size) in enumerate(chunks[1]):
        if group == 0:
            wait_for(came(early), value_sem.at[group], heads * BLK)
        wait_for(came(late), value_sem.at[group], size)
        for head in range(start // BLK, min((start + size) // BLK, first_last)):
            result = acc_ref[head] + jnp.dot(
                weights_ref[head], arrived(values_ref, head), preferred_element_type=jnp.float32
            )
            out_ref[:, head * HD : (head + 1) * HD] = (result * share_ref[head]).astype(out_ref.dtype)

    for slot, (_, up, down, _, _, above) in enumerate(plan):
        sends = down if up is None else up if down is None else None
        whole = 2 * heads * BLK
        if above is None:
            @when(sends)
            def _():
                wait(sent(slot), whole)
            continue

        shorter = down & late
        passes = relays.get(slot, jnp.bool_(False))

        @pl.when(shorter & passes)
        def _():
            wait(sent(slot), whole - skipped + BLK)

        @pl.when(shorter & jnp.logical_not(passes))
        def _():
            wait(sent(slot), whole - skipped)

        plain = jnp.logical_not(shorter)

        @pl.when(plain if sends is None else plain & sends)
        def _():
            wait(sent(slot), whole)


def finish(done_ref, acc_ref, weights_ref, share_ref, values_ref, out_hbm, last_ref, sem):
    width = done_ref.shape[1]
    first = width // HD
    pltpu.make_async_copy(done_ref, out_hbm.at[:, pl.ds(0, width)], sem).start()
    for head in range(acc_ref.shape[0]):
        values = jnp.concatenate(
            [
                values_ref[slot, (first + head) * BLK : (first + head + 1) * BLK]
                for slot in range(values_ref.shape[0])
            ],
            axis=0,
        )
        result = acc_ref[head] + jnp.dot(weights_ref[head], values, preferred_element_type=jnp.float32)
        last_ref[:, head * HD : (head + 1) * HD] = (result * share_ref[head]).astype(last_ref.dtype)
    pltpu.make_async_copy(last_ref, out_hbm.at[:, pl.ds(width, last_ref.shape[1])], sem).start()
    pltpu.make_async_copy(out_hbm, out_hbm, sem).wait()


def per_device(queries, keys, values, adj_mask, border_blocks):
    rows, width = queries.shape[2:]
    heads = width // HD
    clip_count, slab_count, band_count = (lax.axis_size(axis) for axis in ("clip", "tm", "band"))
    sources = (2 if slab_count > 1 else 0) + min(band_count - 1, 2)
    assert rows == 2 * BLK and adj_mask.shape[3] == 2 and border_blocks.shape[3] == 1
    last = last_heads(heads)
    parts = pl.pallas_call(
        functools.partial(kernel, clip_count, slab_count, band_count),
        out_shape=[
            pltpu.VMEM((rows, width - last * HD), jnp.bfloat16),
            pltpu.VMEM((last, rows, HD), jnp.float32),
            pltpu.VMEM((last, rows, sources * BLK), jnp.bfloat16),
            pltpu.VMEM((last, rows, HD), jnp.float32),
            pltpu.VMEM((sources, heads * BLK, HD), jnp.bfloat16),
        ],
        in_specs=[pl.BlockSpec(memory_space=pl.ANY)] * 5,
        out_specs=[pl.BlockSpec(memory_space=pltpu.VMEM)] * 5,
        scratch_shapes=[
            pltpu.VMEM((2 * rows // BLK, BLK, width), jnp.bfloat16),
            pltpu.VMEM((rows // BLK, BLK, width), jnp.bfloat16),
            pltpu.SMEM(adj_mask.shape[2:], jnp.int32),
            pltpu.SMEM(border_blocks.shape[:1:-1], jnp.int32),
            pltpu.VMEM(((sources + 1) * 2 * heads * BLK, HD), jnp.bfloat16),
            pltpu.VMEM((sources, heads * BLK, HD), jnp.bfloat16),
            pltpu.VMEM((heads, rows, HD), jnp.float32),
            pltpu.VMEM((heads, rows, sources * BLK), jnp.bfloat16),
            pltpu.VMEM((heads, rows, HD), jnp.float32),
            pltpu.VMEM((sources, rows // BLK, BLK, HD), jnp.bfloat16),
            pltpu.VMEM((sources, BLK, HD), jnp.bfloat16),
            pltpu.SemaphoreType.DMA((max(4, sources + 1),)),
            pltpu.SemaphoreType.REGULAR,
            pltpu.SemaphoreType.DMA,
            pltpu.SemaphoreType.DMA,
            pltpu.SemaphoreType.DMA,
            pltpu.SemaphoreType.DMA((2,)),
        ],
        compiler_params=pltpu.CompilerParams(
            collective_id=0, has_side_effects=True
        ),
        name="radial_attention",
    )(
        queries.reshape(rows // BLK, BLK, width),
        keys.reshape(rows // BLK, BLK, width),
        values.reshape(rows // BLK, BLK, width),
        adj_mask[0, 0], border_blocks[0, 0].T,
    )
    attended = pl.pallas_call(
        finish,
        out_shape=jax.ShapeDtypeStruct((rows, width), jnp.bfloat16),
        in_specs=[pl.BlockSpec(memory_space=pltpu.VMEM)] * 5,
        out_specs=pl.BlockSpec(memory_space=pl.ANY),
        scratch_shapes=[pltpu.VMEM((rows, last * HD), jnp.bfloat16), pltpu.SemaphoreType.DMA],
        name="last_heads",
    )(*(pltpu.with_memory_space_constraint(part, pltpu.VMEM) for part in parts))
    return attended[None, None]


def solution(mesh):
    placed = (
        P(("clip", "tm"), "band", None, "head"),
        P(("clip", "tm"), "band", None, "head"),
        P(("clip", "tm"), "band", None, "head"),
        P(("clip", "tm"), "band", None, None),
        P(("clip", "tm"), "band", None, None),
    )
    return jax.shard_map(
        per_device,
        mesh=mesh,
        in_specs=placed,
        out_specs=P(("clip", "tm"), "band", None, "head"),
        check_vma=False,
    )
```

```python
import functools
import math

import jax
import jax.numpy as jnp
from jax import lax
from jax.experimental import pallas as pl
from jax.experimental.pallas import tpu as pltpu
from jax.sharding import PartitionSpec as P

BLK = 128
HD = 128

masked_score = -1e30
SCALE2 = math.log2(math.e) / math.sqrt(HD)
MESH = pl.DeviceIdType.MESH
TAIL = 1
LEND_X = 160
LEND_Z = 160

ROUTE_X = ((0, 0, 1), (1, 0, 1))
ROUTE_Z = ((0, 1, 0), (1, 1, 0))


def routes(slab_count, band_count):
    slab, band = lax.axis_index("tm"), lax.axis_index("band")
    found = []
    if slab_count > 1:
        found.append(({"tm": slab - 1}, None, slab > 0, slab < slab_count - 1, ("adj", 1), slab < slab_count - 1))
    if band_count == 2:
        found.append(({"band": 1 - band}, band == 0, band == 1, None, ("border", 1 - band), band == 0))
    elif band_count > 2:
        found.append(({"band": band - 1}, None, band > 0, band < band_count - 1, ("border", 0), band < band_count - 1))
        found.append(({"band": band + 1}, band < band_count - 1, None, band > 0, ("border", 1), None))
    if slab_count > 1:
        found.append(({"tm": slab + 1}, slab < slab_count - 1, None, slab > 0, ("adj", 0), None))
    return found


def when(condition):
    return (lambda body: body()) if condition is None else pl.when(condition)


def last_heads(heads):
    return TAIL if heads > 2 * TAIL else 1


def value_chunks(heads):
    most = heads - last_heads(heads)
    return [(0, most * BLK), (most * BLK, (heads - most) * BLK)]


FLAG = 8


def weigh(query, key):
    scores = lax.dot_general(
        query, key, (((1,), (1,)), ((), ())), preferred_element_type=jnp.float32
    )
    return scores * SCALE2


def kernel(
    clip_count, slab_count, band_count, q_hbm, k_hbm, v_hbm, adj_hbm, border_hbm,
    out_ref, last_acc_ref, last_weights_ref, last_share_ref, values_ref,
    vq_ref, k_ref, adj_ref, border_ref, send_ref, recv_ref, acc_ref, weights_ref, share_ref,
    both_ref, pass_ref,
    load_sem, here_sem, ahead_sem, pass_sem, key_sem, value_sem,
):
    rows, width = k_ref.shape[0] * BLK, k_ref.shape[2]
    loads = [
        pltpu.make_async_copy(source, target, load_sem.at[min(number, 3)])
        for number, (source, target) in enumerate(
            (
                (k_hbm, k_ref), (adj_hbm, adj_ref), (border_hbm, border_ref),
                (v_hbm, vq_ref.at[pl.ds(0, rows // BLK)]), (q_hbm, vq_ref.at[pl.ds(rows // BLK, rows // BLK)]),
            )
        )
    ]
    for load in loads[:3]:
        load.start()

    plan = routes(slab_count, band_count)
    slots = range(len(plan))
    heads = width // HD
    late = lax.axis_index("head") > 0
    early = jnp.logical_not(late)

    neighbours = []
    for axis, count in (("tm", slab_count), ("band", band_count), ("clip", clip_count)):
        if count > 1:
            index = lax.axis_index(axis)
            lower, upper = index > 0, index < count - 1
            if axis == "clip":
                lower, upper = lower & late, upper & late
            neighbours.append((axis, index, lower, upper))

    detours = {}
    if clip_count > 1 and slab_count > 1 and band_count > 1:
        for slot, (_, _, _, _, (kind, _), above) in enumerate(plan):
            if above is not None:
                detours[slot] = ROUTE_X if kind == "border" else ROUTE_Z

    def at(clip, slab, band):
        place = [lax.axis_index(axis) for axis in ("clip", "tm", "band")]
        return (place[0] == clip) & (place[1] == slab) & (place[2] == band) & late

    lends = {slot: at(*source) for slot, (source, _) in detours.items()}
    relays = {slot: at(*middle) for slot, (_, middle) in detours.items()}

    def sent(slot):
        return load_sem.at[slot if slot < 3 else slot + 1]

    def base(slot, part):
        return (slot * 2 + part) * heads * BLK

    def lent(slot):
        return LEND_X if plan[slot][4][0] == "border" else LEND_Z

    def lend(slot):
        return pltpu.make_async_remote_copy(
            src_ref=send_ref.at[pl.ds(base(slot, 1), lent(slot))],
            dst_ref=pass_ref.at[slot, pl.ds(0, lent(slot))],
            send_sem=sent(slot),
            recv_sem=pass_sem,
            device_id=dict(zip(("clip", "tm", "band"), detours[slot][1])),
            device_id_type=MESH,
        )

    def relay(slot):
        return pltpu.make_async_remote_copy(
            src_ref=pass_ref.at[slot, pl.ds(0, lent(slot))],
            dst_ref=values_ref.at[slot, pl.ds(0, lent(slot))],
            send_sem=sent(slot),
            recv_sem=value_sem.at[0],
            device_id={"clip": 0, "tm": 0, "band": 0},
            device_id_type=MESH,
        )

    barrier = pltpu.get_barrier_semaphore()
    for axis, index, _, has_upper in neighbours:
        @pl.when(has_upper)
        def _():
            pl.semaphore_signal(barrier, inc=1, device_id={axis: index + 1}, device_id_type=MESH)

    chunks = [[(0, heads * BLK)], value_chunks(heads)]
    skipped = BLK - FLAG

    def transfer(slot, part, group, skip=0, whole=False):
        start, size = (0, heads * BLK) if whole else chunks[part][group]
        at = pl.ds(start + skip, size - skip)
        return pltpu.make_async_remote_copy(
            src_ref=send_ref.at[pl.ds(base(slot, part) + start + skip, size - skip)],
            dst_ref=values_ref.at[slot, at] if part else recv_ref.at[slot, at],
            send_sem=sent(slot),
            recv_sem=value_sem.at[group] if part else key_sem,
            device_id=plan[slot][0],
            device_id_type=MESH,
        )

    def ahead(slot):
        return pltpu.make_async_remote_copy(
            src_ref=k_hbm.at[:, :, pl.ds(0, HD)],
            dst_ref=both_ref.at[slot],
            send_sem=ahead_sem,
            recv_sem=key_sem,
            device_id=plan[slot][0],
            device_id_type=MESH,
        )

    def wait(sem, size):
        some = send_ref.at[pl.ds(0, size)]
        pltpu.make_async_copy(some, some, sem).wait()

    def wait_for(conditions, sem, size):
        count = sum(jnp.int32(1) if condition is None else condition.astype(jnp.int32) for condition in conditions)
        for number in range(1, len(conditions) + 1):
            @pl.when(count == number)
            def _():
                wait(sem, number * size)

    def send(slot, part, downward):
        _, up, down, _, _, above = plan[slot]
        sends = down if downward else up
        if sends is None:
            return
        for group in range(len(chunks[part])):
            short, skip = late, skipped
            if part:
                short, skip = lends.get(slot), lent(slot)
            if downward and group == 0 and above is not None and short is not None:
                @pl.when(sends & short)
                def _():
                    transfer(slot, part, group, skip).start()

                @pl.when(sends & jnp.logical_not(short))
                def _():
                    transfer(slot, part, group).start()
            else:
                @pl.when(sends)
                def _():
                    transfer(slot, part, group).start()

    arrivals = sum(lower.astype(jnp.int32) for _, _, lower, _ in neighbours)

    @pl.when(arrivals > 0)
    def _():
        pl.semaphore_wait(barrier, arrivals)

    for slot, (_, _, down, _, _, above) in enumerate(plan):
        if above is not None:
            @pl.when(down & late)
            def _():
                ahead(slot).start()

    for axis, index, has_lower, _ in neighbours:
        @pl.when(has_lower)
        def _():
            pl.semaphore_signal(here_sem, inc=1, device_id={axis: index - 1}, device_id_type=MESH)

    for load in loads[3:]:
        load.start()
    for load in loads[:3]:
        load.wait()
    blocks = [
        adj_ref[row, 1] if kind == "adj" else border_ref[0, row] for _, _, _, _, (kind, row), _ in plan
    ]

    def pick(slot, part, whole, start=0):
        for head in range(start, heads):
            to = base(slot, part) + head * BLK
            send_ref[to : to + BLK] = whole[blocks[slot], :, head * HD : (head + 1) * HD]

    def sends(slot):
        _, up, down, _, _, _ = plan[slot]
        return down if up is None else up if down is None else None

    def pick_keys(slot):
        _, _, down, _, _, above = plan[slot]
        if above is None:
            when(sends(slot))(lambda: pick(slot, 0, k_ref))
            return
        when(sends(slot))(lambda: pick(slot, 0, k_ref, 1))
        to = base(slot, 0)

        @pl.when(down & late)
        def _():
            send_ref[to + skipped : to + BLK] = jnp.full((FLAG, HD), blocks[slot].astype(jnp.float32)).astype(jnp.bfloat16)

        @pl.when(jnp.logical_not(down & late))
        def _():
            send_ref[to : to + BLK] = k_ref[blocks[slot], :, :HD]

    for slot in slots:
        pick_keys(slot)
        send(slot, 0, True)
    uppers = sum(upper.astype(jnp.int32) for *_, upper in neighbours)

    @pl.when(uppers > 0)
    def _():
        pl.semaphore_wait(here_sem, uppers)

    for slot in slots:
        send(slot, 0, False)

    pltpu.make_async_copy(vq_ref, vq_ref, load_sem.at[3]).wait()
    for slot in slots:
        when(sends(slot))(functools.partial(pick, slot, 1, vq_ref))
    for slot in detours:
        @pl.when(lends[slot])
        def _():
            lend(slot).start()

    def send_values():
        for slot in slots:
            send(slot, 1, True)
            send(slot, 1, False)

    for slot, (_, up, down, _, _, _) in enumerate(plan):
        @pl.when(early & (down if up is None else up if down is None else up | down))
        def _():
            transfer(slot, 1, 0, whole=True).start()

    for slot, (_, _, _, comes, _, _) in enumerate(plan):
        if comes is not None:
            @pl.when(jnp.logical_not(comes))
            def _():
                recv_ref[slot] = jnp.zeros(recv_ref.shape[1:], recv_ref.dtype)
                values_ref[slot] = jnp.zeros(values_ref.shape[1:], values_ref.dtype)

    first_last = heads - last_acc_ref.shape[0]

    def kept(head):
        if head < first_last:
            return acc_ref.at[head], weights_ref.at[head], share_ref.at[head]
        number = head - first_last
        return last_acc_ref.at[number], last_weights_ref.at[number], last_share_ref.at[number]

    def query(columns):
        return vq_ref[rows // BLK :, :, columns].reshape(rows, HD)

    own = []
    for head in range(heads):
        columns = slice(head * HD, (head + 1) * HD)
        scores = weigh(query(columns), k_ref[:, :, columns].reshape(rows, HD))
        most = jnp.max(scores, axis=1, keepdims=True)
        weights = jnp.exp2(scores - most)
        total = jnp.sum(weights, axis=1, keepdims=True)
        kept(head)[0][...] = jnp.dot(
            weights.astype(jnp.bfloat16), vq_ref[: rows // BLK, :, columns].reshape(rows, HD), preferred_element_type=jnp.float32
        )
        own.append((most, total))

    ones = [above & late for *_, above in plan if above is not None]
    shorter = sum(one.astype(jnp.int32) for one in ones)
    longer = (
        sum(jnp.int32(1) if comes is None else comes.astype(jnp.int32) for _, _, _, comes, _, _ in plan) - shorter
    )
    for some in range(len(ones) + 1):
        for more in range(len(plan) + 1 - some):
            if some + more:
                @pl.when((shorter == some) & (longer == more))
                def _():
                    wait(key_sem, some * (heads * BLK - skipped + rows) + more * heads * BLK)

    for slot, (*_, above) in enumerate(plan):
        if above is not None:
            @pl.when(above & late)
            def _():
                flag = recv_ref[slot, skipped:BLK].astype(jnp.float32)
                recv_ref[slot, :BLK] = jnp.where(
                    jnp.concatenate([flag] * (BLK // FLAG), axis=0) > 0.5,
                    both_ref[slot, 1].astype(jnp.float32),
                    both_ref[slot, 0].astype(jnp.float32),
                ).astype(jnp.bfloat16)

    wait_for([down & late for _, _, down, _, _, above in plan if above is not None], ahead_sem, rows)

    for slot in detours:
        @pl.when(relays[slot])
        def _():
            lend(slot).wait_recv()
            relay(slot).start()

    pl.when(late)(send_values)

    def arrived(ref, head):
        return jnp.concatenate([ref[slot, head * BLK : (head + 1) * BLK] for slot in slots], axis=0)

    hidden = [
        None if comes is None else jnp.where(comes, 0.0, masked_score).astype(jnp.float32)
        for _, _, _, comes, _, _ in plan
    ]
    for head in range(heads):
        columns = slice(head * HD, (head + 1) * HD)
        scores = weigh(query(columns), arrived(recv_ref, head))
        scores = [
            scores[:, slot * BLK : (slot + 1) * BLK] + (0.0 if hidden[slot] is None else hidden[slot]) for slot in slots
        ]
        most, total = own[head]
        largest = jnp.maximum(
            most, jnp.max(functools.reduce(jnp.maximum, scores), axis=1, keepdims=True)
        )
        weights = [jnp.exp2(score - largest) for score in scores]
        factor = jnp.exp2(most - largest)
        share = 1.0 / (factor * total + jnp.sum(sum(weights), axis=1, keepdims=True))
        sum_ref, part_ref, scale_ref = kept(head)
        sum_ref[...] = sum_ref[...] * factor
        scale_ref[...] = jnp.broadcast_to(share, (rows, HD))
        for slot in slots:
            part_ref[:, slot * BLK : (slot + 1) * BLK] = weights[slot].astype(jnp.bfloat16)

    def came(role):
        return [role if comes is None else role & comes for _, _, _, comes, _, _ in plan]

    for group, (start, size) in enumerate(chunks[1]):
        if group == 0:
            wait_for(came(early), value_sem.at[group], heads * BLK)
        wait_for(came(late), value_sem.at[group], size)
        for head in range(start // BLK, min((start + size) // BLK, first_last)):
            result = acc_ref[head] + jnp.dot(
                weights_ref[head], arrived(values_ref, head), preferred_element_type=jnp.float32
            )
            out_ref[:, head * HD : (head + 1) * HD] = (result * share_ref[head]).astype(out_ref.dtype)

    for slot, (_, up, down, _, _, above) in enumerate(plan):
        sends = down if up is None else up if down is None else None
        whole = 2 * heads * BLK
        if above is None:
            @when(sends)
            def _():
                wait(sent(slot), whole)
            continue

        shorter = down & late
        passes = relays.get(slot, jnp.bool_(False))

        @pl.when(shorter & passes)
        def _():
            wait(sent(slot), whole - skipped + lent(slot))

        @pl.when(shorter & jnp.logical_not(passes))
        def _():
            wait(sent(slot), whole - skipped)

        plain = jnp.logical_not(shorter)

        @pl.when(plain if sends is None else plain & sends)
        def _():
            wait(sent(slot), whole)


def finish(done_ref, acc_ref, weights_ref, share_ref, values_ref, out_hbm, last_ref, sem):
    width = done_ref.shape[1]
    first = width // HD
    pltpu.make_async_copy(done_ref, out_hbm.at[:, pl.ds(0, width)], sem).start()
    for head in range(acc_ref.shape[0]):
        values = jnp.concatenate(
            [
                values_ref[slot, (first + head) * BLK : (first + head + 1) * BLK]
                for slot in range(values_ref.shape[0])
            ],
            axis=0,
        )
        result = acc_ref[head] + jnp.dot(weights_ref[head], values, preferred_element_type=jnp.float32)
        last_ref[:, head * HD : (head + 1) * HD] = (result * share_ref[head]).astype(last_ref.dtype)
    pltpu.make_async_copy(last_ref, out_hbm.at[:, pl.ds(width, last_ref.shape[1])], sem).start()
    pltpu.make_async_copy(out_hbm, out_hbm, sem).wait()


def per_device(queries, keys, values, adj_mask, border_blocks):
    rows, width = queries.shape[2:]
    heads = width // HD
    clip_count, slab_count, band_count = (lax.axis_size(axis) for axis in ("clip", "tm", "band"))
    sources = (2 if slab_count > 1 else 0) + min(band_count - 1, 2)
    assert rows == 2 * BLK and adj_mask.shape[3] == 2 and border_blocks.shape[3] == 1
    last = last_heads(heads)
    parts = pl.pallas_call(
        functools.partial(kernel, clip_count, slab_count, band_count),
        out_shape=[
            pltpu.VMEM((rows, width - last * HD), jnp.bfloat16),
            pltpu.VMEM((last, rows, HD), jnp.float32),
            pltpu.VMEM((last, rows, sources * BLK), jnp.bfloat16),
            pltpu.VMEM((last, rows, HD), jnp.float32),
            pltpu.VMEM((sources, heads * BLK, HD), jnp.bfloat16),
        ],
        in_specs=[pl.BlockSpec(memory_space=pl.ANY)] * 5,
        out_specs=[pl.BlockSpec(memory_space=pltpu.VMEM)] * 5,
        scratch_shapes=[
            pltpu.VMEM((2 * rows // BLK, BLK, width), jnp.bfloat16),
            pltpu.VMEM((rows // BLK, BLK, width), jnp.bfloat16),
            pltpu.SMEM(adj_mask.shape[2:], jnp.int32),
            pltpu.SMEM(border_blocks.shape[:1:-1], jnp.int32),
            pltpu.VMEM(((sources + 1) * 2 * heads * BLK, HD), jnp.bfloat16),
            pltpu.VMEM((sources, heads * BLK, HD), jnp.bfloat16),
            pltpu.VMEM((heads, rows, HD), jnp.float32),
            pltpu.VMEM((heads, rows, sources * BLK), jnp.bfloat16),
            pltpu.VMEM((heads, rows, HD), jnp.float32),
            pltpu.VMEM((sources, rows // BLK, BLK, HD), jnp.bfloat16),
            pltpu.VMEM((sources, 2 * BLK, HD), jnp.bfloat16),
            pltpu.SemaphoreType.DMA((max(4, sources + 1),)),
            pltpu.SemaphoreType.REGULAR,
            pltpu.SemaphoreType.DMA,
            pltpu.SemaphoreType.DMA,
            pltpu.SemaphoreType.DMA,
            pltpu.SemaphoreType.DMA((2,)),
        ],
        compiler_params=pltpu.CompilerParams(
            collective_id=0, has_side_effects=True
        ),
        name="radial_attention",
    )(
        queries.reshape(rows // BLK, BLK, width),
        keys.reshape(rows // BLK, BLK, width),
        values.reshape(rows // BLK, BLK, width),
        adj_mask[0, 0], border_blocks[0, 0].T,
    )
    attended = pl.pallas_call(
        finish,
        out_shape=jax.ShapeDtypeStruct((rows, width), jnp.bfloat16),
        in_specs=[pl.BlockSpec(memory_space=pltpu.VMEM)] * 5,
        out_specs=pl.BlockSpec(memory_space=pl.ANY),
        scratch_shapes=[pltpu.VMEM((rows, last * HD), jnp.bfloat16), pltpu.SemaphoreType.DMA],
        name="last_heads",
    )(*(pltpu.with_memory_space_constraint(part, pltpu.VMEM) for part in parts))
    return attended[None, None]


def solution(mesh):
    placed = (
        P(("clip", "tm"), "band", None, "head"),
        P(("clip", "tm"), "band", None, "head"),
        P(("clip", "tm"), "band", None, "head"),
        P(("clip", "tm"), "band", None, None),
        P(("clip", "tm"), "band", None, None),
    )
    return jax.shard_map(
        per_device,
        mesh=mesh,
        in_specs=placed,
        out_specs=P(("clip", "tm"), "band", None, "head"),
        check_vma=False,
    )
```

```python
import functools
import math

import jax
import jax.numpy as jnp
from jax import lax
from jax.experimental import pallas as pl
from jax.experimental.pallas import tpu as pltpu
from jax.sharding import PartitionSpec as P

BLK = 128
HD = 128

masked_score = -1e30
SCALE2 = math.log2(math.e) / math.sqrt(HD)
MESH = pl.DeviceIdType.MESH
TAIL = 1

ROUTE_X = ((0, 0, 1), (1, 0, 1))
ROUTE_Z = ((0, 1, 0), (1, 1, 0))


def routes(slab_count, band_count):
    slab, band = lax.axis_index("tm"), lax.axis_index("band")
    found = []
    if slab_count > 1:
        found.append(({"tm": slab - 1}, None, slab > 0, slab < slab_count - 1, ("adj", 1), slab < slab_count - 1))
    if band_count == 2:
        found.append(({"band": 1 - band}, band == 0, band == 1, None, ("border", 1 - band), band == 0))
    elif band_count > 2:
        found.append(({"band": band - 1}, None, band > 0, band < band_count - 1, ("border", 0), band < band_count - 1))
        found.append(({"band": band + 1}, band < band_count - 1, None, band > 0, ("border", 1), None))
    if slab_count > 1:
        found.append(({"tm": slab + 1}, slab < slab_count - 1, None, slab > 0, ("adj", 0), None))
    return found


def when(condition):
    return (lambda body: body()) if condition is None else pl.when(condition)


def last_heads(heads):
    return TAIL if heads > 2 * TAIL else 1


def value_chunks(heads):
    most = heads - last_heads(heads)
    return [(0, most * BLK), (most * BLK, (heads - most) * BLK)]


FLAG = 8
AHEAD = 80


def weigh(query, key):
    scores = lax.dot_general(
        query, key, (((1,), (1,)), ((), ())), preferred_element_type=jnp.float32
    )
    return scores * SCALE2


def kernel(
    clip_count, slab_count, band_count, q_hbm, k_hbm, v_hbm, adj_hbm, border_hbm,
    out_ref, last_acc_ref, last_weights_ref, last_share_ref, values_ref,
    vq_ref, k_ref, adj_ref, border_ref, send_ref, recv_ref, acc_ref, weights_ref, share_ref,
    both_ref, pass_ref,
    load_sem, here_sem, ahead_sem, pass_sem, key_sem, value_sem,
):
    rows, width = k_ref.shape[0] * BLK, k_ref.shape[2]
    loads = [
        pltpu.make_async_copy(source, target, load_sem.at[min(number, 3)])
        for number, (source, target) in enumerate(
            (
                (k_hbm, k_ref), (adj_hbm, adj_ref), (border_hbm, border_ref),
                (v_hbm, vq_ref.at[pl.ds(0, rows // BLK)]), (q_hbm, vq_ref.at[pl.ds(rows // BLK, rows // BLK)]),
            )
        )
    ]
    for load in loads[:3]:
        load.start()

    plan = routes(slab_count, band_count)
    slots = range(len(plan))
    heads = width // HD
    late = lax.axis_index("head") > 0
    early = jnp.logical_not(late)

    neighbours = []
    for axis, count in (("tm", slab_count), ("band", band_count), ("clip", clip_count)):
        if count > 1:
            index = lax.axis_index(axis)
            lower, upper = index > 0, index < count - 1
            if axis == "clip":
                lower, upper = lower & late, upper & late
            neighbours.append((axis, index, lower, upper))

    detours = {}
    if clip_count > 1 and slab_count > 1 and band_count > 1:
        for slot, (_, _, _, _, (kind, _), above) in enumerate(plan):
            if above is not None:
                detours[slot] = ROUTE_X if kind == "border" else ROUTE_Z

    def at(clip, slab, band):
        place = [lax.axis_index(axis) for axis in ("clip", "tm", "band")]
        return (place[0] == clip) & (place[1] == slab) & (place[2] == band) & late

    lends = {slot: at(*source) for slot, (source, _) in detours.items()}
    relays = {slot: at(*middle) for slot, (_, middle) in detours.items()}

    def sent(slot):
        return load_sem.at[slot if slot < 3 else slot + 1]

    def base(slot, part):
        return (slot * 2 + part) * heads * BLK

    def lend(slot):
        return pltpu.make_async_remote_copy(
            src_ref=send_ref.at[pl.ds(base(slot, 1), BLK)],
            dst_ref=pass_ref.at[slot],
            send_sem=sent(slot),
            recv_sem=pass_sem,
            device_id=dict(zip(("clip", "tm", "band"), detours[slot][1])),
            device_id_type=MESH,
        )

    def relay(slot):
        return pltpu.make_async_remote_copy(
            src_ref=pass_ref.at[slot],
            dst_ref=values_ref.at[slot, pl.ds(0, BLK)],
            send_sem=sent(slot),
            recv_sem=value_sem.at[0],
            device_id={"clip": 0, "tm": 0, "band": 0},
            device_id_type=MESH,
        )

    barrier = pltpu.get_barrier_semaphore()
    for axis, index, _, has_upper in neighbours:
        @pl.when(has_upper)
        def _():
            pl.semaphore_signal(barrier, inc=1, device_id={axis: index + 1}, device_id_type=MESH)

    chunks = [[(0, heads * BLK)], value_chunks(heads)]
    skipped = 2 * AHEAD - FLAG

    def transfer(slot, part, group, skip=0, whole=False):
        start, size = (0, heads * BLK) if whole else chunks[part][group]
        at = pl.ds(start + skip, size - skip)
        return pltpu.make_async_remote_copy(
            src_ref=send_ref.at[pl.ds(base(slot, part) + start + skip, size - skip)],
            dst_ref=values_ref.at[slot, at] if part else recv_ref.at[slot, at],
            send_sem=sent(slot),
            recv_sem=value_sem.at[group] if part else key_sem,
            device_id=plan[slot][0],
            device_id_type=MESH,
        )

    def ahead(slot):
        return pltpu.make_async_remote_copy(
            src_ref=k_hbm.at[:, pl.ds(0, AHEAD), pl.ds(0, 2 * HD)],
            dst_ref=both_ref.at[slot],
            send_sem=ahead_sem,
            recv_sem=key_sem,
            device_id=plan[slot][0],
            device_id_type=MESH,
        )

    def wait(sem, size):
        some = send_ref.at[pl.ds(0, size)]
        pltpu.make_async_copy(some, some, sem).wait()

    def wait_for(conditions, sem, size):
        count = sum(jnp.int32(1) if condition is None else condition.astype(jnp.int32) for condition in conditions)
        for number in range(1, len(conditions) + 1):
            @pl.when(count == number)
            def _():
                wait(sem, number * size)

    def send(slot, part, downward):
        _, up, down, _, _, above = plan[slot]
        sends = down if downward else up
        if sends is None:
            return
        for group in range(len(chunks[part])):
            short, skip = late, skipped
            if part:
                short, skip = lends.get(slot), BLK
            if downward and group == 0 and above is not None and short is not None:
                @pl.when(sends & short)
                def _():
                    transfer(slot, part, group, skip).start()

                @pl.when(sends & jnp.logical_not(short))
                def _():
                    transfer(slot, part, group).start()
            else:
                @pl.when(sends)
                def _():
                    transfer(slot, part, group).start()

    arrivals = sum(lower.astype(jnp.int32) for _, _, lower, _ in neighbours)

    @pl.when(arrivals > 0)
    def _():
        pl.semaphore_wait(barrier, arrivals)

    for slot, (_, _, down, _, _, above) in enumerate(plan):
        if above is not None:
            @pl.when(down & late)
            def _():
                ahead(slot).start()

    for axis, index, has_lower, _ in neighbours:
        @pl.when(has_lower)
        def _():
            pl.semaphore_signal(here_sem, inc=1, device_id={axis: index - 1}, device_id_type=MESH)

    for load in loads[3:]:
        load.start()
    for load in loads[:3]:
        load.wait()
    blocks = [
        adj_ref[row, 1] if kind == "adj" else border_ref[0, row] for _, _, _, _, (kind, row), _ in plan
    ]

    def pick(slot, part, whole, start=0):
        for head in range(start, heads):
            to = base(slot, part) + head * BLK
            send_ref[to : to + BLK] = whole[blocks[slot], :, head * HD : (head + 1) * HD]

    def sends(slot):
        _, up, down, _, _, _ = plan[slot]
        return down if up is None else up if down is None else None

    def pick_keys(slot):
        _, _, down, _, _, above = plan[slot]
        to, block = base(slot, 0), blocks[slot]

        def first():
            for head in range(2):
                send_ref[to + head * AHEAD : to + (head + 1) * AHEAD] = k_ref[
                    block, :AHEAD, head * HD : (head + 1) * HD
                ]

        def rest():
            for head in range(2):
                start = to + 2 * AHEAD + head * (BLK - AHEAD)
                send_ref[start : start + BLK - AHEAD] = k_ref[block, AHEAD:, head * HD : (head + 1) * HD]
            pick(slot, 0, k_ref, 2)

        when(sends(slot))(rest)
        if above is None:
            when(sends(slot))(first)
            return

        @pl.when(down & late)
        def _():
            send_ref[to + skipped : to + 2 * AHEAD] = jnp.full((FLAG, HD), block.astype(jnp.float32)).astype(jnp.bfloat16)

        pl.when(jnp.logical_not(down & late))(first)

    for slot in slots:
        pick_keys(slot)
        send(slot, 0, True)
    uppers = sum(upper.astype(jnp.int32) for *_, upper in neighbours)

    @pl.when(uppers > 0)
    def _():
        pl.semaphore_wait(here_sem, uppers)

    for slot in slots:
        send(slot, 0, False)

    pltpu.make_async_copy(vq_ref, vq_ref, load_sem.at[3]).wait()
    for slot in slots:
        when(sends(slot))(functools.partial(pick, slot, 1, vq_ref))
    for slot in detours:
        @pl.when(lends[slot])
        def _():
            lend(slot).start()

    def send_values():
        for slot in slots:
            send(slot, 1, True)
            send(slot, 1, False)

    for slot, (_, up, down, _, _, _) in enumerate(plan):
        @pl.when(early & (down if up is None else up if down is None else up | down))
        def _():
            transfer(slot, 1, 0, whole=True).start()

    for slot, (_, _, _, comes, _, _) in enumerate(plan):
        if comes is not None:
            @pl.when(jnp.logical_not(comes))
            def _():
                recv_ref[slot] = jnp.zeros(recv_ref.shape[1:], recv_ref.dtype)
                values_ref[slot] = jnp.zeros(values_ref.shape[1:], values_ref.dtype)

    first_last = heads - last_acc_ref.shape[0]

    def kept(head):
        if head < first_last:
            return acc_ref.at[head], weights_ref.at[head], share_ref.at[head]
        number = head - first_last
        return last_acc_ref.at[number], last_weights_ref.at[number], last_share_ref.at[number]

    def query(columns):
        return vq_ref[rows // BLK :, :, columns].reshape(rows, HD)

    own = []
    for head in range(heads):
        columns = slice(head * HD, (head + 1) * HD)
        scores = weigh(query(columns), k_ref[:, :, columns].reshape(rows, HD))
        most = jnp.max(scores, axis=1, keepdims=True)
        weights = jnp.exp2(scores - most)
        total = jnp.sum(weights, axis=1, keepdims=True)
        kept(head)[0][...] = jnp.dot(
            weights.astype(jnp.bfloat16), vq_ref[: rows // BLK, :, columns].reshape(rows, HD), preferred_element_type=jnp.float32
        )
        own.append((most, total))

    ones = [above & late for *_, above in plan if above is not None]
    shorter = sum(one.astype(jnp.int32) for one in ones)
    longer = (
        sum(jnp.int32(1) if comes is None else comes.astype(jnp.int32) for _, _, _, comes, _, _ in plan) - shorter
    )
    for some in range(len(ones) + 1):
        for more in range(len(plan) + 1 - some):
            if some + more:
                @pl.when((shorter == some) & (longer == more))
                def _():
                    wait(key_sem, some * (heads * BLK - skipped + 4 * AHEAD) + more * heads * BLK)

    for slot, (*_, above) in enumerate(plan):
        if above is not None:
            @pl.when(above & late)
            def _():
                flag = recv_ref[slot, skipped : 2 * AHEAD].astype(jnp.float32)
                second = jnp.concatenate([flag] * (AHEAD // FLAG), axis=0) > 0.5
                for head in range(2):
                    columns = slice(head * HD, (head + 1) * HD)
                    recv_ref[slot, head * AHEAD : (head + 1) * AHEAD] = jnp.where(
                        second,
                        both_ref[slot, 1, :, columns].astype(jnp.float32),
                        both_ref[slot, 0, :, columns].astype(jnp.float32),
                    ).astype(jnp.bfloat16)

    wait_for([down & late for _, _, down, _, _, above in plan if above is not None], ahead_sem, 4 * AHEAD)

    for slot in detours:
        @pl.when(relays[slot])
        def _():
            lend(slot).wait_recv()
            relay(slot).start()

    pl.when(late)(send_values)

    def arrived(ref, head):
        return jnp.concatenate([ref[slot, head * BLK : (head + 1) * BLK] for slot in slots], axis=0)

    def arrived_keys(head):
        if head > 1:
            return arrived(recv_ref, head)
        pieces = []
        for slot in slots:
            start = 2 * AHEAD + head * (BLK - AHEAD)
            pieces.append(recv_ref[slot, head * AHEAD : (head + 1) * AHEAD])
            pieces.append(recv_ref[slot, start : start + BLK - AHEAD])
        return jnp.concatenate(pieces, axis=0)

    hidden = [
        None if comes is None else jnp.where(comes, 0.0, masked_score).astype(jnp.float32)
        for _, _, _, comes, _, _ in plan
    ]
    for head in range(heads):
        columns = slice(head * HD, (head + 1) * HD)
        scores = weigh(query(columns), arrived_keys(head))
        scores = [
            scores[:, slot * BLK : (slot + 1) * BLK] + (0.0 if hidden[slot] is None else hidden[slot]) for slot in slots
        ]
        most, total = own[head]
        largest = jnp.maximum(
            most, jnp.max(functools.reduce(jnp.maximum, scores), axis=1, keepdims=True)
        )
        weights = [jnp.exp2(score - largest) for score in scores]
        factor = jnp.exp2(most - largest)
        share = 1.0 / (factor * total + jnp.sum(sum(weights), axis=1, keepdims=True))
        sum_ref, part_ref, scale_ref = kept(head)
        sum_ref[...] = sum_ref[...] * factor
        scale_ref[...] = jnp.broadcast_to(share, (rows, HD))
        for slot in slots:
            part_ref[:, slot * BLK : (slot + 1) * BLK] = weights[slot].astype(jnp.bfloat16)

    def came(role):
        return [role if comes is None else role & comes for _, _, _, comes, _, _ in plan]

    for group, (start, size) in enumerate(chunks[1]):
        if group == 0:
            wait_for(came(early), value_sem.at[group], heads * BLK)
        wait_for(came(late), value_sem.at[group], size)
        for head in range(start // BLK, min((start + size) // BLK, first_last)):
            result = acc_ref[head] + jnp.dot(
                weights_ref[head], arrived(values_ref, head), preferred_element_type=jnp.float32
            )
            out_ref[:, head * HD : (head + 1) * HD] = (result * share_ref[head]).astype(out_ref.dtype)

    for slot, (_, up, down, _, _, above) in enumerate(plan):
        sends = down if up is None else up if down is None else None
        whole = 2 * heads * BLK
        if above is None:
            @when(sends)
            def _():
                wait(sent(slot), whole)
            continue

        shorter = down & late
        passes = relays.get(slot, jnp.bool_(False))

        @pl.when(shorter & passes)
        def _():
            wait(sent(slot), whole - skipped + BLK)

        @pl.when(shorter & jnp.logical_not(passes))
        def _():
            wait(sent(slot), whole - skipped)

        plain = jnp.logical_not(shorter)

        @pl.when(plain if sends is None else plain & sends)
        def _():
            wait(sent(slot), whole)


def finish(done_ref, acc_ref, weights_ref, share_ref, values_ref, out_hbm, last_ref, sem):
    width = done_ref.shape[1]
    first = width // HD
    pltpu.make_async_copy(done_ref, out_hbm.at[:, pl.ds(0, width)], sem).start()
    for head in range(acc_ref.shape[0]):
        values = jnp.concatenate(
            [
                values_ref[slot, (first + head) * BLK : (first + head + 1) * BLK]
                for slot in range(values_ref.shape[0])
            ],
            axis=0,
        )
        result = acc_ref[head] + jnp.dot(weights_ref[head], values, preferred_element_type=jnp.float32)
        last_ref[:, head * HD : (head + 1) * HD] = (result * share_ref[head]).astype(last_ref.dtype)
    pltpu.make_async_copy(last_ref, out_hbm.at[:, pl.ds(width, last_ref.shape[1])], sem).start()
    pltpu.make_async_copy(out_hbm, out_hbm, sem).wait()


def per_device(queries, keys, values, adj_mask, border_blocks):
    rows, width = queries.shape[2:]
    heads = width // HD
    clip_count, slab_count, band_count = (lax.axis_size(axis) for axis in ("clip", "tm", "band"))
    sources = (2 if slab_count > 1 else 0) + min(band_count - 1, 2)
    assert heads > 1 and rows == 2 * BLK and adj_mask.shape[3] == 2 and border_blocks.shape[3] == 1
    last = last_heads(heads)
    parts = pl.pallas_call(
        functools.partial(kernel, clip_count, slab_count, band_count),
        out_shape=[
            pltpu.VMEM((rows, width - last * HD), jnp.bfloat16),
            pltpu.VMEM((last, rows, HD), jnp.float32),
            pltpu.VMEM((last, rows, sources * BLK), jnp.bfloat16),
            pltpu.VMEM((last, rows, HD), jnp.float32),
            pltpu.VMEM((sources, heads * BLK, HD), jnp.bfloat16),
        ],
        in_specs=[pl.BlockSpec(memory_space=pl.ANY)] * 5,
        out_specs=[pl.BlockSpec(memory_space=pltpu.VMEM)] * 5,
        scratch_shapes=[
            pltpu.VMEM((2 * rows // BLK, BLK, width), jnp.bfloat16),
            pltpu.VMEM((rows // BLK, BLK, width), jnp.bfloat16),
            pltpu.SMEM(adj_mask.shape[2:], jnp.int32),
            pltpu.SMEM(border_blocks.shape[:1:-1], jnp.int32),
            pltpu.VMEM(((sources + 1) * 2 * heads * BLK, HD), jnp.bfloat16),
            pltpu.VMEM((sources, heads * BLK, HD), jnp.bfloat16),
            pltpu.VMEM((heads, rows, HD), jnp.float32),
            pltpu.VMEM((heads, rows, sources * BLK), jnp.bfloat16),
            pltpu.VMEM((heads, rows, HD), jnp.float32),
            pltpu.VMEM((sources, rows // BLK, AHEAD, 2 * HD), jnp.bfloat16),
            pltpu.VMEM((sources, BLK, HD), jnp.bfloat16),
            pltpu.SemaphoreType.DMA((max(4, sources + 1),)),
            pltpu.SemaphoreType.REGULAR,
            pltpu.SemaphoreType.DMA,
            pltpu.SemaphoreType.DMA,
            pltpu.SemaphoreType.DMA,
            pltpu.SemaphoreType.DMA((2,)),
        ],
        compiler_params=pltpu.CompilerParams(collective_id=0, has_side_effects=True),
        name="radial_attention",
    )(
        queries.reshape(rows // BLK, BLK, width),
        keys.reshape(rows // BLK, BLK, width),
        values.reshape(rows // BLK, BLK, width),
        adj_mask[0, 0], border_blocks[0, 0].T,
    )
    attended = pl.pallas_call(
        finish,
        out_shape=jax.ShapeDtypeStruct((rows, width), jnp.bfloat16),
        in_specs=[pl.BlockSpec(memory_space=pltpu.VMEM)] * 5,
        out_specs=pl.BlockSpec(memory_space=pl.ANY),
        scratch_shapes=[pltpu.VMEM((rows, last * HD), jnp.bfloat16), pltpu.SemaphoreType.DMA],
        name="last_heads",
    )(*(pltpu.with_memory_space_constraint(part, pltpu.VMEM) for part in parts))
    return attended[None, None]


def solution(mesh):
    placed = (
        P(("clip", "tm"), "band", None, "head"),
        P(("clip", "tm"), "band", None, "head"),
        P(("clip", "tm"), "band", None, "head"),
        P(("clip", "tm"), "band", None, None),
        P(("clip", "tm"), "band", None, None),
    )
    return jax.shard_map(
        per_device,
        mesh=mesh,
        in_specs=placed,
        out_specs=P(("clip", "tm"), "band", None, "head"),
        check_vma=False,
    )
```
